512 devices in a mesh: tok: 64 (over z, y), tp: 8 (over x, core).
Axes of the slice: x: 4, y: 8, z: 8, core: 2. Of those that a mesh axis runs over, the one named last changes fastest.
Arguments:
- activations: bfloat16 [8192, 4096], P('tok', 'tp'), may hold values from -6 to 6
- out_grad: bfloat16 [8192, 4096], P('tok', 'tp'), may hold values from -6 to 6
- routes: int32 [8192, 2], P('tok'), may hold values from 0 to 63, all different within a row; in each aligned block of 128 rows (0 to 127, 128 to 255, ...) at most 8 rows name the same one
- gate_vals: float32 [8192, 2], P('tok'), may hold values from 0.2 to 1
- w_gate: bfloat16 [64, 1536, 4096], P('tok', 'tp'), may hold values from -0.09375 to 0.09375
- w_up: bfloat16 [64, 1536, 4096], P('tok', 'tp'), may hold values from -0.09375 to 0.09375
- w_down: bfloat16 [64, 1536, 4096], P('tok', 'tp'), may hold values from -0.15625 to 0.15625
Outputs:
- in_grad: bfloat16 [8192, 4096], P('tok', 'tp')
The draws below stay inside these ranges and needn't reach their ends.
Inputs may be any that keep to these rules, and one draw needn't show every extreme that they name: `routes`: each row names 2 different experts. In each aligned block of 128 rows (the tokens of one index of tok) no expert is named by more than 8 rows, a bound that some block reaches.
All inputs are finite; a program needn't handle non-finite values.
Results may differ from the reference program's by a relative error of at most 0.0057.
Values may be sent and summed in bfloat16 or wider, within the bound.
No kernel may reach another device: no remote copies, remote signals or barrier semaphores. Data moves between devices by JAX's collectives and lax.ppermute only.
A program may use at most 64 MiB of HBM per device.

```python
import math
import jax
import jax.numpy as jnp
import numpy as np
from jax import lax

D = 4096
FF = 1536
TOP = 2
TOK_DEV = 128
EXPERTS = 64
TOKENS = 8192
CAP_SRC = 8
BUCKET = 512
N_TOK = 64
N_TP = 8


def level_of(own_key, shape, cuts, smallest, largest):
    level = 1.0
    for axis_at, blocks in cuts:
        steps = jax.random.uniform(jax.random.fold_in(jax.random.fold_in(own_key, 6), axis_at), (blocks,), jnp.float32, smallest / len(cuts), largest / len(cuts))
        level = level * jnp.repeat(jnp.exp(steps), shape[axis_at] // blocks).reshape((-1,) + (1,) * (len(shape) - 1 - axis_at))
    return level


def routed_block(rng, own, number, rows, count, top, most, skew):
    sequence = jax.random.permutation(rng, count)
    heavy_load, common = load_shares(count, rows * top, most, skew, True), load_shares(count, rows * top, most, skew, False)
    places = jnp.arange(count)

    def named(sizes, turn):
        used = int((sizes > 0).sum())
        fixed = max(1, used // 4)
        shifted = fixed + (places - fixed + turn * (used - fixed)) % max(1, count - fixed)
        return jnp.zeros((count,), jnp.int32).at[sequence[jnp.where(places < fixed, places, shifted)]].set(jnp.asarray(sizes, jnp.int32))

    sizes = jnp.where(number % 4 == 0, named(heavy_load, number // 4), named(common, number - number // 4 - 1))
    mixed = jax.random.permutation(jax.random.fold_in(own, 3), count)
    giver, receiver = mixed[0:count // 2 * 2:2], mixed[1:count // 2 * 2:2]
    margin = jnp.minimum(sizes[giver] - 1, most - sizes[receiver]) // 2
    margin = jnp.where((giver == sequence[0]) | (receiver == sequence[0]) | (sizes[receiver] == 0), 0, jnp.maximum(margin, 0))
    shifted = jax.random.randint(jax.random.fold_in(own, 4), (count // 2,), 0, 1 << 20) % (margin + 1)
    sizes = sizes.at[giver].add(-shifted).at[receiver].add(shifted)
    labels = jnp.searchsorted(jnp.cumsum(sizes), jnp.arange(rows * top), side="right").astype(jnp.int32)
    table = labels.reshape(top, rows).T
    table = table[jax.random.permutation(jax.random.fold_in(own, 1), rows)]
    turn = jax.random.randint(jax.random.fold_in(own, 2), (rows, 1), 0, top)
    return jnp.take_along_axis(table, (jnp.arange(top)[None, :] + turn) % top, axis=1)


def load_shares(count, total, most, skew, full):
    portions = [(1 << 20) // math.isqrt(rank ** skew) + 1 for rank in range(1, count + 1)]
    largest = most if full else min(most, max(-(-total // count), total * portions[0] // sum(portions)))
    least = 1 if total - largest >= count - 1 else 0
    given, rest = [largest] + [least] * (count - 1), total - largest - least * (count - 1)
    while rest > 0:
        movable = [i for i in range(1, count) if given[i] < largest] or [i for i in range(1, count) if given[i] < most]
        pool, budget = sum([portions[i] for i in movable]), rest
        for i in movable:
            more = min(most - given[i], max(1, budget * portions[i] // pool), rest)
            given[i] = given[i] + more
            rest = rest - more
    return np.array(given)


def scatter_about(stream_key, dims, scale, limit, split=(), kind=jnp.bfloat16):
    array = scale * jax.random.normal(stream_key, dims, jnp.float32)
    if split:
        array = array * level_of(stream_key, dims, split, -0.22, 0.18)
    return jnp.clip(array, -limit, limit).astype(kind)


def setup_inputs(seed: int = 0) -> dict:
    key_list = jax.random.split(jax.random.key(seed), 8)
    activations = scatter_about(key_list[0], (TOKENS, D), 1.0, 6.0, ((0, 64), (1, 8)))
    out_grad = scatter_about(key_list[1], (TOKENS, D), 1.0, 6.0, ((0, 64), (1, 8)))
    routes_keys = jax.random.split(jax.random.fold_in(key_list[2], 1), TOKENS // TOK_DEV)
    routes_turns = jax.random.permutation(jax.random.fold_in(key_list[2], 3), TOKENS // TOK_DEV)
    routes = jax.vmap(lambda own, number: routed_block(jax.random.fold_in(key_list[2], 2), own, number, TOK_DEV, EXPERTS, TOP, CAP_SRC, 2))(routes_keys, routes_turns).reshape((TOKENS, TOP))
    gate_vals = jnp.clip(0.2 + 0.8 * jax.random.uniform(key_list[3], (TOKENS, TOP), jnp.float32) ** level_of(key_list[3], (TOKENS, TOP), ((0, 64),), -0.2, 0.2), 0.2, 1.0)
    w_gate = scatter_about(key_list[4], (EXPERTS, FF, D), D ** -0.5, 0.09375, ((0, 64), (1, 8)))
    w_up = scatter_about(key_list[5], (EXPERTS, FF, D), D ** -0.5, 0.09375, ((0, 64), (1, 8)))
    w_down = scatter_about(key_list[6], (EXPERTS, FF, D), FF ** -0.5, 0.15625, ((0, 64), (1, 8)))
    return {"activations": activations, "out_grad": out_grad, "routes": routes, "gate_vals": gate_vals, "w_gate": w_gate, "w_up": w_up, "w_down": w_down}


def hidden_grads(gate_pre, up_pre, hidden_grad):
    sigma = jax.nn.sigmoid(gate_pre)
    silu_value = gate_pre * sigma
    slope = sigma * (1.0 + gate_pre * (1.0 - sigma))
    return (hidden_grad * up_pre * slope).astype(jnp.bfloat16), (hidden_grad * silu_value).astype(jnp.bfloat16)


def reference(activations, out_grad, routes, gate_vals, w_gate, w_up, w_down):
    experts = N_TOK
    contract_last = (((1,), (1,)), ((), ()))
    per_shard = routes.reshape(N_TOK, TOK_DEV * TOP)
    onehot = (per_shard[:, :, None] == jnp.arange(experts, dtype=jnp.int32)[None, None, :]).astype(jnp.int32)
    before = jnp.cumsum(onehot, axis=1) - onehot
    slot = jnp.sum(before * onehot, axis=2).astype(jnp.int32)
    shard = jnp.arange(N_TOK, dtype=jnp.int32)[:, None]
    flat_index = (per_shard * BUCKET + shard * CAP_SRC + slot).astype(jnp.int32)
    token = (shard * TOK_DEV + (jnp.arange(TOK_DEV * TOP, dtype=jnp.int32) // TOP)[None, :]).astype(jnp.int32)
    table = jnp.full((experts * BUCKET,), TOKENS, jnp.int32)
    table = table.at[flat_index.reshape(-1)].set(token.reshape(-1))
    table = table.reshape(experts, BUCKET)
    padded_x = jnp.concatenate([activations, jnp.zeros((1, D), jnp.bfloat16)], axis=0)
    padded_g = jnp.concatenate([out_grad, jnp.zeros((1, D), jnp.bfloat16)], axis=0)
    ff_dev = FF // N_TP

    def one_expert(operands):
        index, gate_w, up_w, down_w = operands
        rows_x = jnp.take(padded_x, index, axis=0)
        rows_g = jnp.take(padded_g, index, axis=0)
        gate_pre = lax.dot_general(rows_x, gate_w, contract_last, preferred_element_type=jnp.float32)
        up_pre = lax.dot_general(rows_x, up_w, contract_last, preferred_element_type=jnp.float32)
        hidden_grad = lax.dot_general(rows_g, down_w, contract_last, preferred_element_type=jnp.float32)
        gate_grad, up_grad = hidden_grads(gate_pre, up_pre, hidden_grad)
        gate_blocks = gate_grad.astype(jnp.float32).reshape(BUCKET, N_TP, ff_dev)
        up_blocks = up_grad.astype(jnp.float32).reshape(BUCKET, N_TP, ff_dev)
        gate_wide = gate_w.astype(jnp.float32).reshape(N_TP, ff_dev, D)
        up_wide = up_w.astype(jnp.float32).reshape(N_TP, ff_dev, D)
        parts = jnp.einsum("rjf,jfd->jrd", gate_blocks, gate_wide) + jnp.einsum("rjf,jfd->jrd", up_blocks, up_wide)
        rounded = lax.optimization_barrier(parts.astype(jnp.bfloat16)).astype(jnp.float32)
        return jnp.sum(rounded, axis=0)

    sums = lax.map(one_expert, (table, w_gate, w_up, w_down))
    flat_sums = sums.reshape(experts * BUCKET, D)
    picked = jnp.take(flat_sums, flat_index.reshape(-1), axis=0).reshape(TOKENS, TOP, D)
    total = jnp.zeros((TOKENS, D), jnp.float32)
    for column in range(TOP):
        total = total + gate_vals[:, column:column + 1] * picked[:, column]
    return total.astype(jnp.bfloat16)
```

```python
import functools

import jax
import jax.numpy as jnp
from jax import lax
from jax.experimental import pallas as pl
from jax.experimental.pallas import tpu as pltpu
from jax.sharding import PartitionSpec as P

CONTRACT_LAST = (((1,), (1,)), ((), ()))


def dispatch_kernel(n_tok, capacity, routes_ref, gates_ref, x_ref, g_ref, send_x_ref, send_g_ref, hi_ref, lo_ref):
    top_k, tok_dev = routes_ref.shape
    expert = lax.broadcasted_iota(jnp.int32, (n_tok, tok_dev), 0)
    named = jnp.zeros((n_tok, tok_dev), jnp.float32)
    weight = jnp.zeros((n_tok, tok_dev), jnp.float32)
    for k in range(top_k):
        hit = routes_ref[k : k + 1, :] == expert
        named = named + jnp.where(hit, 1.0, 0.0)
        weight = weight + jnp.where(hit, gates_ref[k : k + 1, :], 0.0)
    earlier = lax.broadcasted_iota(jnp.int32, (tok_dev, tok_dev), 0)
    later = lax.broadcasted_iota(jnp.int32, (tok_dev, tok_dev), 1)
    ahead = jnp.where(earlier < later, 1.0, 0.0).astype(jnp.bfloat16)
    before = jnp.dot(named.astype(jnp.bfloat16), ahead, preferred_element_type=jnp.float32)
    rows = n_tok * capacity
    slot = lax.broadcasted_iota(jnp.int32, (n_tok, capacity, tok_dev), 1).astype(jnp.float32)
    at_slot = before[:, None, :] == slot
    placed = jnp.where(at_slot, named[:, None, :], 0.0).reshape(rows, tok_dev)
    scaled = jnp.where(at_slot, weight[:, None, :], 0.0).reshape(rows, tok_dev)
    placed = placed.astype(jnp.bfloat16)
    send_x_ref[...] = jnp.dot(placed, x_ref[...], preferred_element_type=jnp.float32).astype(send_x_ref.dtype)
    send_g_ref[...] = jnp.dot(placed, g_ref[...], preferred_element_type=jnp.float32).astype(send_g_ref.dtype)
    scaled = scaled.T
    high = scaled.astype(jnp.bfloat16)
    hi_ref[...] = high
    lo_ref[...] = (scaled - high.astype(jnp.float32)).astype(jnp.bfloat16)


def dispatch(routes, gate_vals, activations, out_grad, n_tok, capacity):
    tok_dev, width = activations.shape
    rows = n_tok * capacity
    sent = jax.ShapeDtypeStruct((rows, width), activations.dtype)
    mixer = jax.ShapeDtypeStruct((tok_dev, rows), jnp.bfloat16)
    return pl.pallas_call(
        functools.partial(dispatch_kernel, n_tok, capacity),
        out_shape=(sent, sent, mixer, mixer),
        name="dispatch",
    )(routes.T, gate_vals.T, activations, out_grad)


def forward_kernel(x_ref, gate_ref, up_ref, gate_pre_ref, up_pre_ref):
    @pl.when(pl.program_id(0) == 0)
    def _():
        gate_pre_ref[...] = jnp.zeros_like(gate_pre_ref)
        up_pre_ref[...] = jnp.zeros_like(up_pre_ref)

    x = x_ref[...]
    gate_pre_ref[...] += lax.dot_general(x, gate_ref[...], CONTRACT_LAST, preferred_element_type=jnp.float32)
    up_pre_ref[...] += lax.dot_general(x, up_ref[...], CONTRACT_LAST, preferred_element_type=jnp.float32)


def forward(x, w_gate, w_up, steps):
    rows, width = x.shape
    hidden = w_gate.shape[0]
    chunk = width // steps
    by_step = lambda i: (0, i)
    fixed = lambda i: (0, 0)
    pre = jax.ShapeDtypeStruct((rows, hidden), jnp.float32)
    return pl.pallas_call(
        forward_kernel,
        grid=(steps,),
        in_specs=[
            pl.BlockSpec((rows, chunk), by_step),
            pl.BlockSpec((hidden, chunk), by_step),
            pl.BlockSpec((hidden, chunk), by_step),
        ],
        out_specs=[pl.BlockSpec((rows, hidden), fixed)] * 2,
        out_shape=(pre, pre),
        name="forward",
    )(x, w_gate, w_up)


def backward_kernel(steps, g_ref, down_ref, gate_pre_ref, up_pre_ref, gate_ref, up_ref, out_ref, acc_ref, gate_grad_ref, up_grad_ref):
    step = pl.program_id(0)

    @pl.when(step == 0)
    def _():
        acc_ref[...] = jnp.zeros_like(acc_ref)

    @pl.when(step < steps)
    def _():
        acc_ref[...] += lax.dot_general(g_ref[...], down_ref[...], CONTRACT_LAST, preferred_element_type=jnp.float32)

    @pl.when(step == steps - 1)
    def _():
        hidden_grad = acc_ref[...]
        gate_pre = gate_pre_ref[...]
        sigma = 1.0 / (1.0 + jnp.exp(-gate_pre))
        slope = sigma * (1.0 + gate_pre * (1.0 - sigma))
        gate_grad_ref[...] = (hidden_grad * up_pre_ref[...] * slope).astype(jnp.bfloat16)
        up_grad_ref[...] = (hidden_grad * (gate_pre * sigma)).astype(jnp.bfloat16)

    @pl.when(step >= steps)
    def _():
        value = jnp.dot(gate_grad_ref[...], gate_ref[...], preferred_element_type=jnp.float32)
        value = value + jnp.dot(up_grad_ref[...], up_ref[...], preferred_element_type=jnp.float32)
        out_ref[0] = value.astype(out_ref.dtype)


def backward(g, w_down, gate_pre, up_pre, w_gate, w_up, steps, blocks):
    rows, width = g.shape
    hidden = w_down.shape[0]
    chunk = width // steps
    block = width // blocks
    by_step = lambda i: (0, jnp.minimum(i, steps - 1))
    by_block = lambda i: (0, jnp.maximum(i - steps, 0))
    fixed = lambda i: (0, 0)
    return pl.pallas_call(
        functools.partial(backward_kernel, steps),
        grid=(steps + blocks,),
        in_specs=[
            pl.BlockSpec((rows, chunk), by_step),
            pl.BlockSpec((hidden, chunk), by_step),
            pl.BlockSpec((rows, hidden), fixed),
            pl.BlockSpec((rows, hidden), fixed),
            pl.BlockSpec((hidden, block), by_block),
            pl.BlockSpec((hidden, block), by_block),
        ],
        out_specs=pl.BlockSpec((1, rows, block), lambda i: (jnp.maximum(i - steps, 0), 0, 0)),
        out_shape=jax.ShapeDtypeStruct((blocks, rows, block), jnp.bfloat16),
        scratch_shapes=[
            pltpu.VMEM((rows, hidden), jnp.float32),
            pltpu.VMEM((rows, hidden), jnp.bfloat16),
            pltpu.VMEM((rows, hidden), jnp.bfloat16),
        ],
        name="backward",
    )(g, w_down, gate_pre, up_pre, w_gate, w_up)


def combine_kernel(hi_ref, lo_ref, back_ref, out_ref):
    back = back_ref[...]
    total = jnp.dot(hi_ref[...], back, preferred_element_type=jnp.float32)
    total = total + jnp.dot(lo_ref[...], back, preferred_element_type=jnp.float32)
    out_ref[...] = total.astype(out_ref.dtype)


def combine(high, low, back):
    return pl.pallas_call(
        combine_kernel,
        out_shape=jax.ShapeDtypeStruct((high.shape[0], back.shape[1]), jnp.bfloat16),
        name="combine",
    )(high, low, back)


def exchange(rows, n_tok):
    blocks = rows.reshape(n_tok, rows.shape[0] // n_tok, rows.shape[1])
    return lax.all_to_all(blocks, "tok", split_axis=0, concat_axis=0, tiled=True).reshape(rows.shape)


def shards(activations, out_grad, routes, gate_vals, w_gate, w_up, w_down):
    n_tok = lax.axis_size("tok")
    n_tp = lax.axis_size("tp")
    tok_dev, top_k = routes.shape
    capacity = max(2, 2 * tok_dev * top_k // n_tok)
    send_x, send_g, high, low = dispatch(routes, gate_vals, activations, out_grad, n_tok, capacity)
    whole_x = lax.all_gather(exchange(send_x, n_tok), "tp", axis=1, tiled=True)
    whole_g = lax.all_gather(exchange(send_g, n_tok), "tp", axis=1, tiled=True)
    gate_pre, up_pre = forward(whole_x, w_gate[0], w_up[0], 4)
    partial = backward(whole_g, w_down[0], gate_pre, up_pre, w_gate[0], w_up[0], 4, n_tp)
    expert_sum = lax.psum_scatter(partial, "tp", scatter_dimension=0, tiled=False)
    return combine(high, low, exchange(expert_sum, n_tok))


def solution(mesh):
    placed = (
        P("tok", "tp"),
        P("tok", "tp"),
        P("tok", None),
        P("tok", None),
        P("tok", "tp", None),
        P("tok", "tp", None),
        P("tok", "tp", None),
    )
    return jax.shard_map(
        shards, mesh=mesh, in_specs=placed, out_specs=P("tok", "tp"), check_vma=False
    )
```

```python
import functools

import jax
import jax.numpy as jnp
from jax import lax
from jax.experimental import pallas as pl
from jax.experimental.pallas import tpu as pltpu
from jax.sharding import PartitionSpec as P

OFFSETS = (0, 3, 1, 2)
CHIPS = 4
CORES = 2
CONTRACT_LAST = (((1,), (1,)), ((), ()))
CONTRACT_FIRST = (((0,), (0,)), ((), ()))
BIG = pltpu.CompilerParams(vmem_limit_bytes=40 * 1024 * 1024)


def dispatch_kernel(n_tok, capacity, routes_ref, gates_ref, x_ref, g_ref, send_ref, hi_ref, lo_ref):
    top_k, tok_dev = routes_ref.shape
    width = x_ref.shape[1]
    expert = lax.broadcasted_iota(jnp.int32, (n_tok, tok_dev), 0)
    named = jnp.zeros((n_tok, tok_dev), jnp.float32)
    weight = jnp.zeros((n_tok, tok_dev), jnp.float32)
    for k in range(top_k):
        hit = routes_ref[k : k + 1, :] == expert
        named = named + jnp.where(hit, 1.0, 0.0)
        weight = weight + jnp.where(hit, gates_ref[k : k + 1, :], 0.0)
    earlier = lax.broadcasted_iota(jnp.int32, (tok_dev, tok_dev), 0)
    later = lax.broadcasted_iota(jnp.int32, (tok_dev, tok_dev), 1)
    ahead = jnp.where(earlier < later, 1.0, 0.0).astype(jnp.bfloat16)
    before = jnp.dot(named.astype(jnp.bfloat16), ahead, preferred_element_type=jnp.float32)
    rows = n_tok * capacity
    slot = lax.broadcasted_iota(jnp.int32, (n_tok, capacity, tok_dev), 1).astype(jnp.float32)
    at_slot = before[:, None, :] == slot
    placed = jnp.where(at_slot, named[:, None, :], 0.0).reshape(rows, tok_dev)
    scaled = jnp.where(at_slot, weight[:, None, :], 0.0).reshape(rows, tok_dev)
    placed = placed.astype(jnp.bfloat16)
    send_ref[:, :width] = jnp.dot(placed, x_ref[...], preferred_element_type=jnp.float32).astype(send_ref.dtype)
    send_ref[:, width:] = jnp.dot(placed, g_ref[...], preferred_element_type=jnp.float32).astype(send_ref.dtype)
    scaled = scaled.T
    high = scaled.astype(jnp.bfloat16)
    hi_ref[...] = high
    lo_ref[...] = (scaled - high.astype(jnp.float32)).astype(jnp.bfloat16)


def dispatch(routes, gate_vals, activations, out_grad, n_tok, capacity):
    tok_dev, width = activations.shape
    rows = n_tok * capacity
    mixer = jax.ShapeDtypeStruct((tok_dev, rows), jnp.bfloat16)
    return pl.pallas_call(
        functools.partial(dispatch_kernel, n_tok, capacity),
        out_shape=(jax.ShapeDtypeStruct((rows, 2 * width), activations.dtype), mixer, mixer),
        name="dispatch",
    )(routes.T, gate_vals.T, activations, out_grad)


def pack_kernel(blocks_ref, *refs):
    keep_ref, give_ref = refs[6:]
    hidden = refs[0].shape[0]
    for n in range(3):
        keep_ref[0, n * hidden : (n + 1) * hidden, :] = refs[n][...]
        give_ref[0, n * hidden : (n + 1) * hidden, :] = refs[3 + n][...]


def pack(blocks, weights):
    hidden, width = weights[0].shape
    block = width // (CHIPS * CORES)
    packed = jax.ShapeDtypeStruct((CHIPS, 3 * hidden, block), weights[0].dtype)
    keep = pl.BlockSpec((hidden, block), lambda i, blocks_ref: (0, blocks_ref[i]))
    give = pl.BlockSpec((hidden, block), lambda i, blocks_ref: (0, blocks_ref[i + CHIPS]))
    out = pl.BlockSpec((1, 3 * hidden, block), lambda i, blocks_ref: (i, 0, 0))
    return pl.pallas_call(
        pack_kernel,
        grid_spec=pltpu.PrefetchScalarGridSpec(
            num_scalar_prefetch=1,
            grid=(CHIPS,),
            in_specs=[keep] * 3 + [give] * 3,
            out_specs=[out, out],
        ),
        out_shape=(packed, packed),
        name="pack",
    )(blocks, *weights, *weights)


def products(weight, rows):
    block = weight.shape[1]
    split = weight.shape[0] // 3 * 2
    wide = lax.dot_general(weight[:split], rows[:, :block], CONTRACT_LAST, preferred_element_type=jnp.float32)
    narrow = lax.dot_general(weight[split:], rows[:, block:], CONTRACT_LAST, preferred_element_type=jnp.float32)
    return wide, narrow, split


def first_kernel(own_ref, left_ref, right_ref, keep_ref, sib_ref, out_ref):
    for n, weights in enumerate((keep_ref, sib_ref)):
        wide, narrow = 0.0, 0.0
        for r, rows in enumerate((own_ref, left_ref, right_ref)):
            a, b, split = products(weights[r], rows[...])
            wide, narrow = wide + a, narrow + b
        out_ref[n, :split, :] = wide
        out_ref[n, split:, :] = narrow


def first(own, left, right, keep, sib):
    rows, width = own.shape
    _, depth, block = keep.shape
    half = rows // 2
    by_half = pl.BlockSpec((half, width), lambda i: (i, 0))
    weights = pl.BlockSpec((CHIPS - 1, depth, block), lambda i: (0, 0, 0))
    return pl.pallas_call(
        first_kernel,
        grid=(2,),
        in_specs=[by_half] * 3 + [weights] * 2,
        out_specs=pl.BlockSpec((CORES, depth, half), lambda i: (0, 0, i)),
        out_shape=jax.ShapeDtypeStruct((CORES, depth, rows), jnp.float32),
        compiler_params=BIG,
        name="first",
    )(own, left, right, keep, sib)


def second_kernel(low_ref, high_ref, keep_ref, sib_ref, sum_ref, out_ref):
    def add(rows_ref):
        for n, weights in enumerate((keep_ref, sib_ref)):
            wide, narrow, split = products(weights[0], rows_ref[...])
            out_ref[n, :split, :] = sum_ref[n, :split, :] + wide
            out_ref[n, split:, :] = sum_ref[n, split:, :] + narrow

    @pl.when(pl.program_id(0) == 0)
    def _():
        add(low_ref)

    @pl.when(pl.program_id(0) == 1)
    def _():
        add(high_ref)


def second(low, high, keep, sib, sums):
    half, width = low.shape
    _, depth, block = keep.shape
    whole = pl.BlockSpec((half, width), lambda i: (0, 0))
    weights = pl.BlockSpec((1, depth, block), lambda i: (CHIPS - 1, 0, 0))
    by_half = pl.BlockSpec((CORES, depth, half), lambda i: (0, 0, i))
    return pl.pallas_call(
        second_kernel,
        grid=(2,),
        in_specs=[whole] * 2 + [weights] * 2 + [by_half],
        out_specs=by_half,
        out_shape=jax.ShapeDtypeStruct(sums.shape, sums.dtype),
        compiler_params=BIG,
        name="second",
    )(low, high, keep, sib, sums)


def chip_sum(grads_ref, keep_ref, sib_ref):
    depth = grads_ref.shape[1]
    return jnp.dot(grads_ref[0].T, keep_ref[0, :depth, :], preferred_element_type=jnp.float32) + jnp.dot(
        grads_ref[1].T, sib_ref[0, :depth, :], preferred_element_type=jnp.float32
    )


def grads_kernel(mine_ref, theirs_ref, keep_ref, sib_ref, grads_ref, low_ref, high_ref):
    hidden = mine_ref.shape[1] // 3
    for n in range(CORES):
        gate_pre = mine_ref[n, :hidden, :] + theirs_ref[1 - n, :hidden, :]
        up_pre = mine_ref[n, hidden : 2 * hidden, :] + theirs_ref[1 - n, hidden : 2 * hidden, :]
        hidden_grad = mine_ref[n, 2 * hidden :, :] + theirs_ref[1 - n, 2 * hidden :, :]
        sigma = 1.0 / (1.0 + jnp.exp(-gate_pre))
        slope = sigma * (1.0 + gate_pre * (1.0 - sigma))
        grads_ref[n, :hidden, :] = (hidden_grad * up_pre * slope).astype(grads_ref.dtype)
        grads_ref[n, hidden:, :] = (hidden_grad * (gate_pre * sigma)).astype(grads_ref.dtype)
    value = chip_sum(grads_ref, keep_ref, sib_ref).astype(low_ref.dtype)

    @pl.when(pl.program_id(0) == 0)
    def _():
        low_ref[...] = value

    @pl.when(pl.program_id(0) == 1)
    def _():
        high_ref[...] = value


def grads(mine, theirs, keep, sib):
    _, depth, rows = mine.shape
    block = keep.shape[2]
    half = rows // 2
    wide = depth // 3 * 2
    by_half = pl.BlockSpec((CORES, depth, half), lambda i: (0, 0, i))
    weights = pl.BlockSpec((1, depth, block), lambda i: (CHIPS - 1, 0, 0))
    whole = pl.BlockSpec((half, block), lambda i: (0, 0))
    part = jax.ShapeDtypeStruct((half, block), jnp.bfloat16)
    return pl.pallas_call(
        grads_kernel,
        grid=(2,),
        in_specs=[by_half] * 2 + [weights] * 2,
        out_specs=[pl.BlockSpec((CORES, wide, half), lambda i: (0, 0, i)), whole, whole],
        out_shape=(jax.ShapeDtypeStruct((CORES, wide, rows), jnp.bfloat16), part, part),
        compiler_params=BIG,
        name="grads",
    )(mine, theirs, keep, sib)


def sides_kernel(grads_ref, keep_left_ref, sib_left_ref, keep_right_ref, sib_right_ref, low_ref, high_ref, left_ref, right_ref):
    to_left = chip_sum(grads_ref, keep_left_ref, sib_left_ref)
    to_right = chip_sum(grads_ref, keep_right_ref, sib_right_ref)

    @pl.when(pl.program_id(0) == 0)
    def _():
        left_ref[...] = to_left.astype(left_ref.dtype)
        right_ref[...] = (to_right + low_ref[...].astype(jnp.float32)).astype(right_ref.dtype)

    @pl.when(pl.program_id(0) == 1)
    def _():
        left_ref[...] = (to_left + high_ref[...].astype(jnp.float32)).astype(left_ref.dtype)
        right_ref[...] = to_right.astype(right_ref.dtype)


def sides(grads_value, keep, sib, low, high):
    _, wide, rows = grads_value.shape
    _, depth, block = keep.shape
    half = rows // 2
    left = pl.BlockSpec((1, depth, block), lambda i: (1, 0, 0))
    right = pl.BlockSpec((1, depth, block), lambda i: (2, 0, 0))
    whole = pl.BlockSpec((half, block), lambda i: (0, 0))
    by_half = pl.BlockSpec((half, block), lambda i: (i, 0))
    out = jax.ShapeDtypeStruct((rows, block), jnp.bfloat16)
    return pl.pallas_call(
        sides_kernel,
        grid=(2,),
        in_specs=[pl.BlockSpec((CORES, wide, half), lambda i: (0, 0, i)), left, left, right, right, whole, whole],
        out_specs=[by_half] * 2,
        out_shape=(out, out),
        compiler_params=BIG,
        name="sides",
    )(grads_value, keep, sib, keep, sib, low, high)


def total_kernel(grads_ref, keep_ref, sib_ref, a_ref, b_ref, out_ref):
    value = chip_sum(grads_ref, keep_ref, sib_ref)
    value = value + a_ref[...].astype(jnp.float32) + b_ref[...].astype(jnp.float32)
    out_ref[...] = value.astype(out_ref.dtype)


def total(grads_value, keep, sib, a, b):
    _, wide, rows = grads_value.shape
    _, depth, block = keep.shape
    half = rows // 2
    own = pl.BlockSpec((1, depth, block), lambda i: (0, 0, 0))
    by_half = pl.BlockSpec((half, block), lambda i: (i, 0))
    return pl.pallas_call(
        total_kernel,
        grid=(2,),
        in_specs=[pl.BlockSpec((CORES, wide, half), lambda i: (0, 0, i)), own, own, by_half, by_half],
        out_specs=by_half,
        out_shape=jax.ShapeDtypeStruct((rows, block), jnp.bfloat16),
        compiler_params=BIG,
        name="total",
    )(grads_value, keep, sib, a, b)


def combine_kernel(hi_ref, lo_ref, back_ref, out_ref):
    back = back_ref[...]
    value = jnp.dot(hi_ref[...], back, preferred_element_type=jnp.float32)
    value = value + jnp.dot(lo_ref[...], back, preferred_element_type=jnp.float32)
    out_ref[...] = value.astype(out_ref.dtype)


def combine(high, low, back):
    return pl.pallas_call(
        combine_kernel,
        out_shape=jax.ShapeDtypeStruct((high.shape[0], back.shape[1]), jnp.bfloat16),
        name="combine",
    )(high, low, back)


def exchange(rows, n_tok):
    blocks = rows.reshape(n_tok, rows.shape[0] // n_tok, rows.shape[1])
    return lax.all_to_all(blocks, "tok", split_axis=0, concat_axis=0, tiled=True).reshape(rows.shape)


def send(value, to):
    return lax.ppermute(value, "tp", [(i, to(i)) for i in range(CHIPS * CORES)])


def to_right(value):
    return send(value, lambda i: (i + CORES) % (CHIPS * CORES))


def to_left(value):
    return send(value, lambda i: (i - CORES) % (CHIPS * CORES))


def to_sibling(value):
    return send(value, lambda i: i ^ 1)


def expert(own, weights):
    place = lax.axis_index("tp").astype(jnp.int32)
    chip, core = place >> 1, place & 1
    keep_blocks = ((chip + jnp.array(OFFSETS, jnp.int32)) & (CHIPS - 1)) * CORES + core
    blocks = jnp.concatenate([keep_blocks, keep_blocks ^ 1])
    keep, give = pack(blocks, weights)
    sib = to_sibling(give)
    left, right = to_right(own), to_left(own)
    half = own.shape[0] // 2
    opposite_low, opposite_high = to_right(left[:half]), to_left(right[half:])
    mine = first(own, left, right, keep, sib)
    mine = second(opposite_low, opposite_high, keep, sib, mine)
    theirs = to_sibling(mine)
    grads_value, part_low, part_high = grads(mine, theirs, keep, sib)
    got_low, got_high = to_right(part_low), to_left(part_high)
    for_left, for_right = sides(grads_value, keep, sib, got_low, got_high)
    from_left, from_right = to_right(for_right), to_left(for_left)
    return total(grads_value, keep, sib, from_left, from_right)


def shards(activations, out_grad, routes, gate_vals, w_gate, w_up, w_down):
    n_tok = lax.axis_size("tok")
    tok_dev, top_k = routes.shape
    capacity = max(2, 2 * tok_dev * top_k // n_tok)
    sent, high, low = dispatch(routes, gate_vals, activations, out_grad, n_tok, capacity)
    weights, sent = lax.optimization_barrier(((w_gate[0], w_up[0], w_down[0]), sent))
    expert_sum = expert(exchange(sent, n_tok), weights)
    return combine(high, low, exchange(expert_sum, n_tok))


def solution(mesh):
    placed = (
        P("tok", "tp"),
        P("tok", "tp"),
        P("tok", None),
        P("tok", None),
        P("tok", "tp", None),
        P("tok", "tp", None),
        P("tok", "tp", None),
    )
    return jax.shard_map(
        shards, mesh=mesh, in_specs=placed, out_specs=P("tok", "tp"), check_vma=False
    )
```

```python
import functools

import jax
import jax.numpy as jnp
from jax import lax
from jax.experimental import pallas as pl
from jax.experimental.pallas import tpu as pltpu
from jax.sharding import PartitionSpec as P

OFFSETS = (0, 3, 1, 2)
CHIPS = 4
CORES = 2
CONTRACT_LAST = (((1,), (1,)), ((), ()))
CONTRACT_FIRST = (((0,), (0,)), ((), ()))
BIG = pltpu.CompilerParams(vmem_limit_bytes=40 * 1024 * 1024)


def dispatch_kernel(n_tok, capacity, routes_ref, gates_ref, x_ref, g_ref, send_ref, hi_ref, lo_ref):
    top_k, tok_dev = routes_ref.shape
    width = x_ref.shape[1]
    expert = lax.broadcasted_iota(jnp.int32, (n_tok, tok_dev), 0)
    named = jnp.zeros((n_tok, tok_dev), jnp.float32)
    weight = jnp.zeros((n_tok, tok_dev), jnp.float32)
    for k in range(top_k):
        hit = routes_ref[k : k + 1, :] == expert
        named = named + jnp.where(hit, 1.0, 0.0)
        weight = weight + jnp.where(hit, gates_ref[k : k + 1, :], 0.0)
    earlier = lax.broadcasted_iota(jnp.int32, (tok_dev, tok_dev), 0)
    later = lax.broadcasted_iota(jnp.int32, (tok_dev, tok_dev), 1)
    ahead = jnp.where(earlier < later, 1.0, 0.0).astype(jnp.bfloat16)
    before = jnp.dot(named.astype(jnp.bfloat16), ahead, preferred_element_type=jnp.float32)
    rows = n_tok * capacity
    slot = lax.broadcasted_iota(jnp.int32, (n_tok, capacity, tok_dev), 1).astype(jnp.float32)
    at_slot = before[:, None, :] == slot
    placed = jnp.where(at_slot, named[:, None, :], 0.0).reshape(rows, tok_dev)
    scaled = jnp.where(at_slot, weight[:, None, :], 0.0).reshape(rows, tok_dev)
    placed = placed.astype(jnp.bfloat16)
    send_ref[:, :width] = jnp.dot(placed, x_ref[...], preferred_element_type=jnp.float32).astype(send_ref.dtype)
    send_ref[:, width:] = jnp.dot(placed, g_ref[...], preferred_element_type=jnp.float32).astype(send_ref.dtype)
    scaled = scaled.T
    high = scaled.astype(jnp.bfloat16)
    hi_ref[...] = high
    lo_ref[...] = (scaled - high.astype(jnp.float32)).astype(jnp.bfloat16)


def dispatch(routes, gate_vals, activations, out_grad, n_tok, capacity):
    tok_dev, width = activations.shape
    rows = n_tok * capacity
    mixer = jax.ShapeDtypeStruct((tok_dev, rows), jnp.bfloat16)
    return pl.pallas_call(
        functools.partial(dispatch_kernel, n_tok, capacity),
        out_shape=(jax.ShapeDtypeStruct((rows, 2 * width), activations.dtype), mixer, mixer),
        name="dispatch",
    )(routes.T, gate_vals.T, activations, out_grad)


def pack_kernel(blocks_ref, *refs):
    keep_ref, give_ref = refs[6:]
    hidden = refs[0].shape[0]
    for n in range(3):
        keep_ref[0, n * hidden : (n + 1) * hidden, :] = refs[n][...]
        give_ref[0, n * hidden : (n + 1) * hidden, :] = refs[3 + n][...]


def pack(blocks, weights):
    hidden, width = weights[0].shape
    block = width // (CHIPS * CORES)
    packed = jax.ShapeDtypeStruct((CHIPS, 3 * hidden, block), weights[0].dtype)
    keep = pl.BlockSpec((hidden, block), lambda i, blocks_ref: (0, blocks_ref[i]))
    give = pl.BlockSpec((hidden, block), lambda i, blocks_ref: (0, blocks_ref[i + CHIPS]))
    out = pl.BlockSpec((1, 3 * hidden, block), lambda i, blocks_ref: (i, 0, 0))
    return pl.pallas_call(
        pack_kernel,
        grid_spec=pltpu.PrefetchScalarGridSpec(
            num_scalar_prefetch=1,
            grid=(CHIPS,),
            in_specs=[keep] * 3 + [give] * 3,
            out_specs=[out, out],
        ),
        out_shape=(packed, packed),
        name="pack",
    )(blocks, *weights, *weights)


def products(weight, rows):
    block = weight.shape[1]
    split = weight.shape[0] // 3 * 2
    wide = lax.dot_general(weight[:split], rows[:, :block], CONTRACT_LAST, preferred_element_type=jnp.float32)
    narrow = lax.dot_general(weight[split:], rows[:, block:], CONTRACT_LAST, preferred_element_type=jnp.float32)
    return wide, narrow, split


def first_kernel(own_ref, left_low_ref, left_high_ref, right_low_ref, right_high_ref, keep_ref, sib_ref, out_ref):
    def add(left_ref, right_ref):
        for n, weights in enumerate((keep_ref, sib_ref)):
            wide, narrow = 0.0, 0.0
            for r, rows in enumerate((own_ref, left_ref, right_ref)):
                a, b, split = products(weights[r], rows[...])
                wide, narrow = wide + a, narrow + b
            out_ref[n, :split, :] = wide
            out_ref[n, split:, :] = narrow

    @pl.when(pl.program_id(0) == 0)
    def _():
        add(left_low_ref, right_low_ref)

    @pl.when(pl.program_id(0) == 1)
    def _():
        add(left_high_ref, right_high_ref)


def first(own, left, right, keep, sib):
    rows, width = own.shape
    _, depth, block = keep.shape
    half = rows // 2
    whole = pl.BlockSpec((half, width), lambda i: (0, 0))
    weights = pl.BlockSpec((CHIPS - 1, depth, block), lambda i: (0, 0, 0))
    return pl.pallas_call(
        first_kernel,
        grid=(2,),
        in_specs=[pl.BlockSpec((half, width), lambda i: (i, 0))] + [whole] * 4 + [weights] * 2,
        out_specs=pl.BlockSpec((CORES, depth, half), lambda i: (0, 0, i)),
        out_shape=jax.ShapeDtypeStruct((CORES, depth, rows), jnp.float32),
        compiler_params=BIG,
        name="first",
    )(own, *left, *right, keep, sib)


def second_kernel(low_ref, high_ref, keep_ref, sib_ref, sum_ref, out_ref):
    def add(rows_ref):
        for n, weights in enumerate((keep_ref, sib_ref)):
            wide, narrow, split = products(weights[0], rows_ref[...])
            out_ref[n, :split, :] = sum_ref[n, :split, :] + wide
            out_ref[n, split:, :] = sum_ref[n, split:, :] + narrow

    @pl.when(pl.program_id(0) == 0)
    def _():
        add(low_ref)

    @pl.when(pl.program_id(0) == 1)
    def _():
        add(high_ref)


def second(low, high, keep, sib, sums):
    half, width = low.shape
    _, depth, block = keep.shape
    whole = pl.BlockSpec((half, width), lambda i: (0, 0))
    weights = pl.BlockSpec((1, depth, block), lambda i: (CHIPS - 1, 0, 0))
    by_half = pl.BlockSpec((CORES, depth, half), lambda i: (0, 0, i))
    return pl.pallas_call(
        second_kernel,
        grid=(2,),
        in_specs=[whole] * 2 + [weights] * 2 + [by_half],
        out_specs=by_half,
        out_shape=jax.ShapeDtypeStruct(sums.shape, sums.dtype),
        compiler_params=BIG,
        name="second",
    )(low, high, keep, sib, sums)


def chip_sum(grads, keep, sib):
    depth = grads.shape[1]
    return jnp.dot(grads[0].T, keep[:depth, :], preferred_element_type=jnp.float32) + jnp.dot(
        grads[1].T, sib[:depth, :], preferred_element_type=jnp.float32
    )


def grads_kernel(mine_ref, theirs_ref, keep_ref, sib_ref, grads_ref, opposite_low_ref, opposite_high_ref, left_low_ref, right_high_ref):
    hidden = mine_ref.shape[1] // 3
    for n in range(CORES):
        gate_pre = mine_ref[n, :hidden, :] + theirs_ref[1 - n, :hidden, :]
        up_pre = mine_ref[n, hidden : 2 * hidden, :] + theirs_ref[1 - n, hidden : 2 * hidden, :]
        hidden_grad = mine_ref[n, 2 * hidden :, :] + theirs_ref[1 - n, 2 * hidden :, :]
        sigma = 1.0 / (1.0 + jnp.exp(-gate_pre))
        slope = sigma * (1.0 + gate_pre * (1.0 - sigma))
        grads_ref[n, :hidden, :] = (hidden_grad * up_pre * slope).astype(grads_ref.dtype)
        grads_ref[n, hidden:, :] = (hidden_grad * (gate_pre * sigma)).astype(grads_ref.dtype)

    def store(out_ref, block):
        out_ref[...] = chip_sum(grads_ref[...], keep_ref[block], sib_ref[block]).astype(out_ref.dtype)

    @pl.when(pl.program_id(0) == 0)
    def _():
        store(opposite_low_ref, 3)
        store(left_low_ref, 1)

    @pl.when(pl.program_id(0) == 1)
    def _():
        store(opposite_high_ref, 3)
        store(right_high_ref, 2)


def grads(mine, theirs, keep, sib):
    _, depth, rows = mine.shape
    block = keep.shape[2]
    half = rows // 2
    wide = depth // 3 * 2
    by_half = pl.BlockSpec((CORES, depth, half), lambda i: (0, 0, i))
    weights = pl.BlockSpec(keep.shape, lambda i: (0, 0, 0))
    whole = pl.BlockSpec((half, block), lambda i: (0, 0))
    part = jax.ShapeDtypeStruct((half, block), jnp.bfloat16)
    return pl.pallas_call(
        grads_kernel,
        grid=(2,),
        in_specs=[by_half] * 2 + [weights] * 2,
        out_specs=[pl.BlockSpec((CORES, wide, half), lambda i: (0, 0, i))] + [whole] * 4,
        out_shape=(jax.ShapeDtypeStruct((CORES, wide, rows), jnp.bfloat16),) + (part,) * 4,
        compiler_params=BIG,
        name="grads",
    )(mine, theirs, keep, sib)


def sides_kernel(grads_low_ref, grads_high_ref, keep_ref, sib_ref, low_ref, high_ref, right_low_ref, left_high_ref):
    value = chip_sum(grads_low_ref[...], keep_ref[1], sib_ref[1]) + low_ref[...].astype(jnp.float32)
    right_low_ref[...] = value.astype(right_low_ref.dtype)
    value = chip_sum(grads_high_ref[...], keep_ref[0], sib_ref[0]) + high_ref[...].astype(jnp.float32)
    left_high_ref[...] = value.astype(left_high_ref.dtype)


def sides(grads_value, keep, sib, low, high):
    _, wide, rows = grads_value.shape
    _, depth, block = keep.shape
    half = rows // 2
    weights = pl.BlockSpec((pl.Element(2), pl.Element(depth), pl.Element(block)), lambda i: (1, 0, 0))
    whole = pl.BlockSpec((half, block), lambda i: (0, 0))
    out = jax.ShapeDtypeStruct((half, block), jnp.bfloat16)
    return pl.pallas_call(
        sides_kernel,
        grid=(1,),
        in_specs=[
            pl.BlockSpec((CORES, wide, half), lambda i: (0, 0, 0)),
            pl.BlockSpec((CORES, wide, half), lambda i: (0, 0, 1)),
            weights,
            weights,
            whole,
            whole,
        ],
        out_specs=[whole] * 2,
        out_shape=(out, out),
        compiler_params=BIG,
        name="sides",
    )(grads_value, grads_value, keep, sib, low, high)


def total_kernel(grads_ref, keep_ref, sib_ref, a_low_ref, a_high_ref, b_low_ref, b_high_ref, out_ref):
    value = chip_sum(grads_ref[...], keep_ref[0], sib_ref[0])

    def store(a_ref, b_ref):
        out_ref[...] = (value + a_ref[...].astype(jnp.float32) + b_ref[...].astype(jnp.float32)).astype(out_ref.dtype)

    @pl.when(pl.program_id(0) == 0)
    def _():
        store(a_low_ref, b_low_ref)

    @pl.when(pl.program_id(0) == 1)
    def _():
        store(a_high_ref, b_high_ref)


def total(grads_value, keep, sib, a, b):
    _, wide, rows = grads_value.shape
    _, depth, block = keep.shape
    half = rows // 2
    own = pl.BlockSpec((1, depth, block), lambda i: (0, 0, 0))
    whole = pl.BlockSpec((half, block), lambda i: (0, 0))
    return pl.pallas_call(
        total_kernel,
        grid=(2,),
        in_specs=[pl.BlockSpec((CORES, wide, half), lambda i: (0, 0, i)), own, own] + [whole] * 4,
        out_specs=pl.BlockSpec((half, block), lambda i: (i, 0)),
        out_shape=jax.ShapeDtypeStruct((rows, block), jnp.bfloat16),
        compiler_params=BIG,
        name="total",
    )(grads_value, keep, sib, *a, *b)


def combine_kernel(hi_ref, lo_ref, back_ref, out_ref):
    back = back_ref[...]
    value = jnp.dot(hi_ref[...], back, preferred_element_type=jnp.float32)
    value = value + jnp.dot(lo_ref[...], back, preferred_element_type=jnp.float32)
    out_ref[...] = value.astype(out_ref.dtype)


def combine(high, low, back):
    return pl.pallas_call(
        combine_kernel,
        out_shape=jax.ShapeDtypeStruct((high.shape[0], back.shape[1]), jnp.bfloat16),
        name="combine",
    )(high, low, back)


def exchange(rows, n_tok):
    blocks = rows.reshape(n_tok, rows.shape[0] // n_tok, rows.shape[1])
    return lax.all_to_all(blocks, "tok", split_axis=0, concat_axis=0, tiled=True).reshape(rows.shape)


def send(value, to):
    return lax.ppermute(value, "tp", [(i, to(i)) for i in range(CHIPS * CORES)])


def to_right(value):
    return send(value, lambda i: (i + CORES) % (CHIPS * CORES))


def to_left(value):
    return send(value, lambda i: (i - CORES) % (CHIPS * CORES))


def to_sibling(value):
    return send(value, lambda i: i ^ 1)


def expert(own, weights):
    place = lax.axis_index("tp").astype(jnp.int32)
    chip, core = place >> 1, place & 1
    keep_blocks = ((chip + jnp.array(OFFSETS, jnp.int32)) & (CHIPS - 1)) * CORES + core
    blocks = jnp.concatenate([keep_blocks, keep_blocks ^ 1])
    keep, give = pack(blocks, weights)
    sib = to_sibling(give)
    half = own.shape[0] // 2
    low, high = own[:half], own[half:]
    left_low, right_high = to_right(low), to_left(high)
    left_high, right_low = to_right(high), to_left(low)
    opposite_low, opposite_high = to_right(left_low), to_left(right_high)
    mine = first(own, (left_low, left_high), (right_low, right_high), keep, sib)
    mine = second(opposite_low, opposite_high, keep, sib, mine)
    theirs = to_sibling(mine)
    grads_value, part_low, part_high, for_left_low, for_right_high = grads(mine, theirs, keep, sib)
    got_low, got_high = to_right(part_low), to_left(part_high)
    from_left_high, from_right_low = to_right(for_right_high), to_left(for_left_low)
    for_right_low, for_left_high = sides(grads_value, keep, sib, got_low, got_high)
    from_left_low, from_right_high = to_right(for_right_low), to_left(for_left_high)
    return total(grads_value, keep, sib, (from_left_low, from_left_high), (from_right_low, from_right_high))


def shards(activations, out_grad, routes, gate_vals, w_gate, w_up, w_down):
    n_tok = lax.axis_size("tok")
    tok_dev, top_k = routes.shape
    capacity = max(2, 2 * tok_dev * top_k // n_tok)
    sent, high, low = dispatch(routes, gate_vals, activations, out_grad, n_tok, capacity)
    weights, sent = lax.optimization_barrier(((w_gate[0], w_up[0], w_down[0]), sent))
    expert_sum = expert(exchange(sent, n_tok), weights)
    return combine(high, low, exchange(expert_sum, n_tok))


def solution(mesh):
    placed = (
        P("tok", "tp"),
        P("tok", "tp"),
        P("tok", None),
        P("tok", None),
        P("tok", "tp", None),
        P("tok", "tp", None),
        P("tok", "tp", None),
    )
    return jax.shard_map(
        shards, mesh=mesh, in_specs=placed, out_specs=P("tok", "tp"), check_vma=False
    )
```

```python
import functools

import jax
import jax.numpy as jnp
from jax import lax
from jax.experimental import pallas as pl
from jax.experimental.pallas import tpu as pltpu
from jax.sharding import PartitionSpec as P

CHIPS = 4
CORES = 2
CONTRACT_LAST = (((1,), (1,)), ((), ()))
BIG = pltpu.CompilerParams(vmem_limit_bytes=40 * 1024 * 1024)


def places(routes_ref, values, n_tok, capacity):
    top_k, tok_dev = routes_ref.shape
    expert = lax.broadcasted_iota(jnp.int32, (n_tok, tok_dev), 0)
    named = jnp.zeros((n_tok, tok_dev), jnp.float32)
    weight = jnp.zeros((n_tok, tok_dev), jnp.float32)
    for k in range(top_k):
        hit = routes_ref[k : k + 1, :] == expert
        named = named + jnp.where(hit, 1.0, 0.0)
        weight = weight + jnp.where(hit, values[k], 0.0)
    earlier = lax.broadcasted_iota(jnp.int32, (tok_dev, tok_dev), 0)
    later = lax.broadcasted_iota(jnp.int32, (tok_dev, tok_dev), 1)
    ahead = jnp.where(earlier < later, 1.0, 0.0).astype(jnp.bfloat16)
    before = jnp.dot(named.astype(jnp.bfloat16), ahead, preferred_element_type=jnp.float32)
    before = jnp.where(named > 0.0, before, -1.0)
    slot = lax.broadcasted_iota(jnp.int32, (n_tok, capacity, tok_dev), 1).astype(jnp.float32)
    placed = jnp.where(before[:, None, :] == slot, weight[:, None, :], 0.0)
    return placed.reshape(n_tok * capacity, tok_dev)


def dispatch_kernel(n_tok, capacity, routes_ref, x_ref, g_ref, send_ref):
    width = x_ref.shape[1]
    placed = places(routes_ref, (1.0,) * routes_ref.shape[0], n_tok, capacity).astype(jnp.bfloat16)
    send_ref[:, :width] = jnp.dot(placed, x_ref[...], preferred_element_type=jnp.float32).astype(send_ref.dtype)
    send_ref[:, width:] = jnp.dot(placed, g_ref[...], preferred_element_type=jnp.float32).astype(send_ref.dtype)


def dispatch(routes, activations, out_grad, n_tok, capacity):
    width = activations.shape[1]
    return pl.pallas_call(
        functools.partial(dispatch_kernel, n_tok, capacity),
        out_shape=jax.ShapeDtypeStruct((n_tok * capacity, 2 * width), activations.dtype),
        name="dispatch",
    )(routes.T, activations, out_grad)


def mixer_kernel(n_tok, capacity, routes_ref, gates_ref, hi_ref, lo_ref):
    gates = [gates_ref[k : k + 1, :] for k in range(gates_ref.shape[0])]
    scaled = places(routes_ref, gates, n_tok, capacity).T
    high = scaled.astype(jnp.bfloat16)
    hi_ref[...] = high
    lo_ref[...] = (scaled - high.astype(jnp.float32)).astype(jnp.bfloat16)


def mixer(routes, gate_vals, n_tok, capacity):
    part = jax.ShapeDtypeStruct((routes.shape[0], n_tok * capacity), jnp.bfloat16)
    return pl.pallas_call(
        functools.partial(mixer_kernel, n_tok, capacity),
        out_shape=(part, part),
        name="mixer",
    )(routes.T, gate_vals.T)


def pack_kernel(blocks_ref, *refs):
    keep_ref, give_ref = refs[6:]
    hidden = refs[0].shape[0]
    for n in range(3):
        keep_ref[0, n * hidden : (n + 1) * hidden, :] = refs[n][...]
        give_ref[0, n * hidden : (n + 1) * hidden, :] = refs[3 + n][...]


def pack(blocks, weights):
    hidden, width = weights[0].shape
    block = width // (CHIPS * CORES)
    packed = jax.ShapeDtypeStruct((CHIPS, 3 * hidden, block), weights[0].dtype)
    keep = pl.BlockSpec((hidden, block), lambda i, blocks_ref: (0, blocks_ref[i]))
    give = pl.BlockSpec((hidden, block), lambda i, blocks_ref: (0, blocks_ref[i + CHIPS]))
    out = pl.BlockSpec((1, 3 * hidden, block), lambda i, blocks_ref: (i, 0, 0))
    return pl.pallas_call(
        pack_kernel,
        grid_spec=pltpu.PrefetchScalarGridSpec(
            num_scalar_prefetch=1,
            grid=(CHIPS,),
            in_specs=[keep] * 3 + [give] * 3,
            out_specs=[out, out],
        ),
        out_shape=(packed, packed),
        name="pack",
    )(blocks, *weights, *weights)


def products(weight, rows):
    block = weight.shape[1]
    split = weight.shape[0] // 3 * 2
    wide = lax.dot_general(weight[:split], rows[:, :block], CONTRACT_LAST, preferred_element_type=jnp.float32)
    narrow = lax.dot_general(weight[split:], rows[:, block:], CONTRACT_LAST, preferred_element_type=jnp.float32)
    return wide, narrow, split


def first_kernel(own_ref, same_ref, other_ref, keep_ref, sib_ref, out_ref):
    for n, weights in enumerate((keep_ref, sib_ref)):
        wide, narrow = 0.0, 0.0
        for r, rows in enumerate((own_ref, same_ref, other_ref)):
            a, b, split = products(weights[r], rows[...])
            wide, narrow = wide + a, narrow + b
        out_ref[n, :split, :] = wide
        out_ref[n, split:, :] = narrow


def first(own, same, other, keep, sib):
    rows, width = own.shape
    _, depth, block = keep.shape
    half = rows // 2
    weights = pl.BlockSpec((CHIPS - 1, depth, block), lambda i: (0, 0, 0))
    return pl.pallas_call(
        first_kernel,
        grid=(2,),
        in_specs=[pl.BlockSpec((half, width), lambda i: (i, 0))] * 3 + [weights] * 2,
        out_specs=pl.BlockSpec((CORES, depth, half), lambda i: (0, 0, i)),
        out_shape=jax.ShapeDtypeStruct((CORES, depth, rows), jnp.float32),
        compiler_params=BIG,
        name="first",
    )(own, same, other, keep, sib)


def second_kernel(rows_ref, keep_ref, sib_ref, sum_ref, out_ref):
    for n, weights in enumerate((keep_ref, sib_ref)):
        wide, narrow, split = products(weights[0], rows_ref[...])
        out_ref[n, :split, :] = sum_ref[n, :split, :] + wide
        out_ref[n, split:, :] = sum_ref[n, split:, :] + narrow


def second(opposite, keep, sib, sums):
    rows, width = opposite.shape
    _, depth, block = keep.shape
    half = rows // 2
    weights = pl.BlockSpec((1, depth, block), lambda i: (CHIPS - 1, 0, 0))
    by_half = pl.BlockSpec((CORES, depth, half), lambda i: (0, 0, i))
    return pl.pallas_call(
        second_kernel,
        grid=(2,),
        in_specs=[pl.BlockSpec((half, width), lambda i: (i, 0))] + [weights] * 2 + [by_half],
        out_specs=by_half,
        out_shape=jax.ShapeDtypeStruct(sums.shape, sums.dtype),
        compiler_params=BIG,
        name="second",
    )(opposite, keep, sib, sums)


def chip_sum(grads, keep, sib):
    depth = grads.shape[1]
    return jnp.dot(grads[0].T, keep[:depth, :], preferred_element_type=jnp.float32) + jnp.dot(
        grads[1].T, sib[:depth, :], preferred_element_type=jnp.float32
    )


def grads_kernel(mine_ref, theirs_ref, keep_ref, sib_ref, grads_ref, opposite_ref, other_ref):
    hidden = mine_ref.shape[1] // 3
    for n in range(CORES):
        gate_pre = mine_ref[n, :hidden, :] + theirs_ref[1 - n, :hidden, :]
        up_pre = mine_ref[n, hidden : 2 * hidden, :] + theirs_ref[1 - n, hidden : 2 * hidden, :]
        hidden_grad = mine_ref[n, 2 * hidden :, :] + theirs_ref[1 - n, 2 * hidden :, :]
        sigma = 1.0 / (1.0 + jnp.exp(-gate_pre))
        slope = sigma * (1.0 + gate_pre * (1.0 - sigma))
        grads_ref[n, :hidden, :] = (hidden_grad * up_pre * slope).astype(grads_ref.dtype)
        grads_ref[n, hidden:, :] = (hidden_grad * (gate_pre * sigma)).astype(grads_ref.dtype)
    opposite_ref[...] = chip_sum(grads_ref[...], keep_ref[1], sib_ref[1]).astype(opposite_ref.dtype)
    other_ref[...] = chip_sum(grads_ref[...], keep_ref[0], sib_ref[0]).astype(other_ref.dtype)


def grads(mine, theirs, keep, sib):
    _, depth, rows = mine.shape
    block = keep.shape[2]
    half = rows // 2
    wide = depth // 3 * 2
    by_half = pl.BlockSpec((CORES, depth, half), lambda i: (0, 0, i))
    weights = pl.BlockSpec((2, depth, block), lambda i: (1, 0, 0))
    part = jax.ShapeDtypeStruct((rows, block), jnp.bfloat16)
    return pl.pallas_call(
        grads_kernel,
        grid=(2,),
        in_specs=[by_half] * 2 + [weights] * 2,
        out_specs=[pl.BlockSpec((CORES, wide, half), lambda i: (0, 0, i))] + [pl.BlockSpec((half, block), lambda i: (i, 0))] * 2,
        out_shape=(jax.ShapeDtypeStruct((CORES, wide, rows), jnp.bfloat16), part, part),
        compiler_params=BIG,
        name="grads",
    )(mine, theirs, keep, sib)


def add_kernel(grads_ref, keep_ref, sib_ref, *refs):
    value = chip_sum(grads_ref[...], keep_ref[0], sib_ref[0])
    for got_ref in refs[:-1]:
        value = value + got_ref[...].astype(jnp.float32)
    refs[-1][...] = value.astype(refs[-1].dtype)


def add(grads_value, keep, sib, got, at):
    _, wide, rows = grads_value.shape
    _, depth, block = keep.shape
    half = rows // 2
    weights = pl.BlockSpec((1, depth, block), lambda i: (at, 0, 0))
    by_half = pl.BlockSpec((half, block), lambda i: (i, 0))
    return pl.pallas_call(
        add_kernel,
        grid=(2,),
        in_specs=[pl.BlockSpec((CORES, wide, half), lambda i: (0, 0, i)), weights, weights] + [by_half] * len(got),
        out_specs=by_half,
        out_shape=jax.ShapeDtypeStruct((rows, block), jnp.bfloat16),
        compiler_params=BIG,
        name="add",
    )(grads_value, keep, sib, *got)


def combine_kernel(hi_ref, lo_ref, back_ref, out_ref):
    back = back_ref[...]
    value = jnp.dot(hi_ref[...], back, preferred_element_type=jnp.float32)
    value = value + jnp.dot(lo_ref[...], back, preferred_element_type=jnp.float32)
    out_ref[...] = value.astype(out_ref.dtype)


def combine(high, low, back):
    return pl.pallas_call(
        combine_kernel,
        out_shape=jax.ShapeDtypeStruct((high.shape[0], back.shape[1]), jnp.bfloat16),
        name="combine",
    )(high, low, back)


def exchange(rows, n_tok):
    blocks = rows.reshape(n_tok, rows.shape[0] // n_tok, rows.shape[1])
    return lax.all_to_all(blocks, "tok", split_axis=0, concat_axis=0, tiled=True).reshape(rows.shape)


def send(value, to):
    pairs = []
    for i in range(CHIPS * CORES):
        chip, core = to(i // CORES, i % CORES)
        pairs.append((i, chip % CHIPS * CORES + core))
    return lax.ppermute(value, "tp", pairs)


def from_near(value):
    return send(value, lambda chip, core: (chip + 1 - 2 * core, core))


def to_near(value):
    return send(value, lambda chip, core: (chip - 1 + 2 * core, core))


def to_near_other(value):
    return send(value, lambda chip, core: (chip - 1 + 2 * core, 1 - core))


def to_sibling(value):
    return send(value, lambda chip, core: (chip, 1 - core))


def block_order(chip, core):
    near = chip - 1 + 2 * core
    chips = jnp.stack([chip, near, near, chip + 2]) & (CHIPS - 1)
    return chips * CORES + jnp.stack([core, core, 1 - core, core])


def expert(own, weights):
    place = lax.axis_index("tp").astype(jnp.int32)
    chip, core = place >> 1, place & 1
    keep, give = pack(jnp.concatenate([block_order(chip, core), block_order(chip, 1 - core)]), weights)
    sib = to_sibling(give)
    same = from_near(own)
    other = to_near_other(own)
    opposite = from_near(same)
    mine = first(own, same, other, keep, sib)
    mine = second(opposite, keep, sib, mine)
    theirs = to_sibling(mine)
    grads_value, for_opposite, for_other = grads(mine, theirs, keep, sib)
    passing = to_near(for_opposite)
    from_other = to_near_other(for_other)
    from_far = to_near(add(grads_value, keep, sib, (passing,), 1))
    return add(grads_value, keep, sib, (from_far, from_other), 0)


def shards(activations, out_grad, routes, gate_vals, w_gate, w_up, w_down):
    n_tok = lax.axis_size("tok")
    tok_dev, top_k = routes.shape
    capacity = max(2, 2 * tok_dev * top_k // n_tok)
    sent = dispatch(routes, activations, out_grad, n_tok, capacity)
    weights, sent, gate_vals = lax.optimization_barrier(((w_gate[0], w_up[0], w_down[0]), sent, gate_vals))
    high, low = mixer(routes, gate_vals, n_tok, capacity)
    expert_sum = expert(exchange(sent, n_tok), weights)
    return combine(high, low, exchange(expert_sum, n_tok))


def solution(mesh):
    placed = (
        P("tok", "tp"),
        P("tok", "tp"),
        P("tok", None),
        P("tok", None),
        P("tok", "tp", None),
        P("tok", "tp", None),
        P("tok", "tp", None),
    )
    return jax.shard_map(
        shards, mesh=mesh, in_specs=placed, out_specs=P("tok", "tp"), check_vma=False
    )
```

```python
import functools

import jax
import jax.numpy as jnp
from jax import lax
from jax.experimental import pallas as pl
from jax.experimental.pallas import tpu as pltpu
from jax.sharding import PartitionSpec as P

CHIPS = 4
CORES = 2
CONTRACT_LAST = (((1,), (1,)), ((), ()))
BIG = pltpu.CompilerParams(vmem_limit_bytes=40 * 1024 * 1024)


def places(routes_ref, values, n_tok, capacity):
    top_k, tok_dev = routes_ref.shape
    expert = lax.broadcasted_iota(jnp.int32, (n_tok, tok_dev), 0)
    named = jnp.zeros((n_tok, tok_dev), jnp.float32)
    weight = jnp.zeros((n_tok, tok_dev), jnp.float32)
    for k in range(top_k):
        hit = routes_ref[k : k + 1, :] == expert
        named = named + jnp.where(hit, 1.0, 0.0)
        weight = weight + jnp.where(hit, values[k], 0.0)
    earlier = lax.broadcasted_iota(jnp.int32, (tok_dev, tok_dev), 0)
    later = lax.broadcasted_iota(jnp.int32, (tok_dev, tok_dev), 1)
    ahead = jnp.where(earlier < later, 1.0, 0.0).astype(jnp.bfloat16)
    before = jnp.dot(named.astype(jnp.bfloat16), ahead, preferred_element_type=jnp.float32)
    before = jnp.where(named > 0.0, before, -1.0)
    slot = lax.broadcasted_iota(jnp.int32, (n_tok, capacity, tok_dev), 1).astype(jnp.float32)
    placed = jnp.where(before[:, None, :] == slot, weight[:, None, :], 0.0)
    return placed.reshape(n_tok * capacity, tok_dev)


def dispatch_kernel(n_tok, capacity, routes_ref, x_ref, g_ref, send_ref):
    width = x_ref.shape[1]
    placed = places(routes_ref, (1.0,) * routes_ref.shape[0], n_tok, capacity).astype(jnp.bfloat16)
    send_ref[:, :width] = jnp.dot(placed, x_ref[...], preferred_element_type=jnp.float32).astype(send_ref.dtype)
    send_ref[:, width:] = jnp.dot(placed, g_ref[...], preferred_element_type=jnp.float32).astype(send_ref.dtype)


def dispatch(routes, activations, out_grad, n_tok, capacity):
    width = activations.shape[1]
    return pl.pallas_call(
        functools.partial(dispatch_kernel, n_tok, capacity),
        out_shape=jax.ShapeDtypeStruct((n_tok * capacity, 2 * width), activations.dtype),
        name="dispatch",
    )(routes.T, activations, out_grad)


def mixer_kernel(n_tok, capacity, routes_ref, gates_ref, hi_ref, lo_ref):
    gates = [gates_ref[k : k + 1, :] for k in range(gates_ref.shape[0])]
    scaled = places(routes_ref, gates, n_tok, capacity).T
    high = scaled.astype(jnp.bfloat16)
    hi_ref[...] = high
    lo_ref[...] = (scaled - high.astype(jnp.float32)).astype(jnp.bfloat16)


def mixer(routes, gate_vals, n_tok, capacity):
    part = jax.ShapeDtypeStruct((routes.shape[0], n_tok * capacity), jnp.bfloat16)
    return pl.pallas_call(
        functools.partial(mixer_kernel, n_tok, capacity),
        out_shape=(part, part),
        name="mixer",
    )(routes.T, gate_vals.T)


def pack_kernel(blocks_ref, *refs):
    keep_ref, give_ref = refs[6:]
    hidden = refs[0].shape[0]
    for n in range(3):
        keep_ref[0, n * hidden : (n + 1) * hidden, :] = refs[n][...]
        give_ref[0, n * hidden : (n + 1) * hidden, :] = refs[3 + n][...]


def pack(blocks, weights):
    hidden, width = weights[0].shape
    block = width // (CHIPS * CORES)
    packed = jax.ShapeDtypeStruct((CHIPS, 3 * hidden, block), weights[0].dtype)
    keep = pl.BlockSpec((hidden, block), lambda i, blocks_ref: (0, blocks_ref[i]))
    give = pl.BlockSpec((hidden, block), lambda i, blocks_ref: (0, blocks_ref[i + CHIPS]))
    out = pl.BlockSpec((1, 3 * hidden, block), lambda i, blocks_ref: (i, 0, 0))
    return pl.pallas_call(
        pack_kernel,
        grid_spec=pltpu.PrefetchScalarGridSpec(
            num_scalar_prefetch=1,
            grid=(CHIPS,),
            in_specs=[keep] * 3 + [give] * 3,
            out_specs=[out, out],
        ),
        out_shape=(packed, packed),
        name="pack",
    )(blocks, *weights, *weights)


def products(weight, rows):
    block = weight.shape[1]
    split = weight.shape[0] // 3 * 2
    wide = lax.dot_general(weight[:split], rows[:, :block], CONTRACT_LAST, preferred_element_type=jnp.float32)
    narrow = lax.dot_general(weight[split:], rows[:, block:], CONTRACT_LAST, preferred_element_type=jnp.float32)
    return wide, narrow, split


def first_kernel(own_ref, same_low_ref, same_high_ref, keep_ref, sib_ref, out_ref):
    def store(same_ref):
        for n, weights in enumerate((keep_ref, sib_ref)):
            wide, narrow, split = products(weights[0], own_ref[...])
            same_wide, same_narrow, _ = products(weights[1], same_ref[...])
            out_ref[n, :split, :] = wide + same_wide
            out_ref[n, split:, :] = narrow + same_narrow

    @pl.when(pl.program_id(0) == 0)
    def _():
        store(same_low_ref)

    @pl.when(pl.program_id(0) == 1)
    def _():
        store(same_high_ref)


def first(own, same_low, same_high, keep, sib):
    rows, width = own.shape
    _, depth, block = keep.shape
    half = rows // 2
    whole = pl.BlockSpec((half, width), lambda i: (0, 0))
    weights = pl.BlockSpec((2, depth, block), lambda i: (0, 0, 0))
    return pl.pallas_call(
        first_kernel,
        grid=(2,),
        in_specs=[pl.BlockSpec((half, width), lambda i: (i, 0)), whole, whole, weights, weights],
        out_specs=pl.BlockSpec((CORES, depth, half), lambda i: (0, 0, i)),
        out_shape=jax.ShapeDtypeStruct((CORES, depth, rows), jnp.float32),
        compiler_params=BIG,
        name="first",
    )(own, same_low, same_high, keep, sib)


def second_kernel(other_ref, low_ref, high_ref, keep_ref, sib_ref, sum_ref, out_ref):
    def add(rows_ref):
        for n, weights in enumerate((keep_ref, sib_ref)):
            wide, narrow, split = products(weights[0], other_ref[...])
            far_wide, far_narrow, _ = products(weights[1], rows_ref[...])
            out_ref[n, :split, :] = sum_ref[n, :split, :] + (wide + far_wide)
            out_ref[n, split:, :] = sum_ref[n, split:, :] + (narrow + far_narrow)

    @pl.when(pl.program_id(0) == 0)
    def _():
        add(low_ref)

    @pl.when(pl.program_id(0) == 1)
    def _():
        add(high_ref)


def second(other, low, high, keep, sib, sums):
    half, width = low.shape
    _, depth, block = keep.shape
    whole = pl.BlockSpec((half, width), lambda i: (0, 0))
    weights = pl.BlockSpec((2, depth, block), lambda i: (1, 0, 0))
    by_half = pl.BlockSpec((CORES, depth, half), lambda i: (0, 0, i))
    return pl.pallas_call(
        second_kernel,
        grid=(2,),
        in_specs=[pl.BlockSpec((half, width), lambda i: (i, 0)), whole, whole, weights, weights, by_half],
        out_specs=by_half,
        out_shape=jax.ShapeDtypeStruct(sums.shape, sums.dtype),
        compiler_params=BIG,
        name="second",
    )(other, low, high, keep, sib, sums)


def chip_sum(grads, keep, sib):
    depth = grads.shape[1]
    return jnp.dot(grads[0].T, keep[:depth, :], preferred_element_type=jnp.float32) + jnp.dot(
        grads[1].T, sib[:depth, :], preferred_element_type=jnp.float32
    )


def grads_kernel(mine_ref, theirs_ref, keep_ref, sib_ref, grads_ref, opposite_ref, other_ref):
    hidden = mine_ref.shape[1] // 3
    for n in range(CORES):
        gate_pre = mine_ref[n, :hidden, :] + theirs_ref[1 - n, :hidden, :]
        up_pre = mine_ref[n, hidden : 2 * hidden, :] + theirs_ref[1 - n, hidden : 2 * hidden, :]
        hidden_grad = mine_ref[n, 2 * hidden :, :] + theirs_ref[1 - n, 2 * hidden :, :]
        sigma = 1.0 / (1.0 + jnp.exp(-gate_pre))
        slope = sigma * (1.0 + gate_pre * (1.0 - sigma))
        grads_ref[n, :hidden, :] = (hidden_grad * up_pre * slope).astype(grads_ref.dtype)
        grads_ref[n, hidden:, :] = (hidden_grad * (gate_pre * sigma)).astype(grads_ref.dtype)
    opposite_ref[...] = chip_sum(grads_ref[...], keep_ref[1], sib_ref[1]).astype(opposite_ref.dtype)
    other_ref[...] = chip_sum(grads_ref[...], keep_ref[0], sib_ref[0]).astype(other_ref.dtype)


def grads(mine, theirs, keep, sib):
    _, depth, rows = mine.shape
    block = keep.shape[2]
    half = rows // 2
    wide = depth // 3 * 2
    by_half = pl.BlockSpec((CORES, depth, half), lambda i: (0, 0, i))
    weights = pl.BlockSpec((2, depth, block), lambda i: (1, 0, 0))
    part = jax.ShapeDtypeStruct((rows, block), jnp.bfloat16)
    return pl.pallas_call(
        grads_kernel,
        grid=(2,),
        in_specs=[by_half] * 2 + [weights] * 2,
        out_specs=[pl.BlockSpec((CORES, wide, half), lambda i: (0, 0, i))] + [pl.BlockSpec((half, block), lambda i: (i, 0))] * 2,
        out_shape=(jax.ShapeDtypeStruct((CORES, wide, rows), jnp.bfloat16), part, part),
        compiler_params=BIG,
        name="grads",
    )(mine, theirs, keep, sib)


def add_kernel(grads_ref, keep_ref, sib_ref, *refs):
    value = chip_sum(grads_ref[...], keep_ref[0], sib_ref[0])
    for got_ref in refs[:-1]:
        value = value + got_ref[...].astype(jnp.float32)
    refs[-1][...] = value.astype(refs[-1].dtype)


def add(grads_value, keep, sib, got, at):
    _, wide, rows = grads_value.shape
    _, depth, block = keep.shape
    half = rows // 2
    weights = pl.BlockSpec((1, depth, block), lambda i: (at, 0, 0))
    by_half = pl.BlockSpec((half, block), lambda i: (i, 0))
    return pl.pallas_call(
        add_kernel,
        grid=(2,),
        in_specs=[pl.BlockSpec((CORES, wide, half), lambda i: (0, 0, i)), weights, weights] + [by_half] * len(got),
        out_specs=by_half,
        out_shape=jax.ShapeDtypeStruct((rows, block), jnp.bfloat16),
        compiler_params=BIG,
        name="add",
    )(grads_value, keep, sib, *got)


def combine_kernel(hi_ref, lo_ref, back_ref, out_ref):
    back = back_ref[...]
    value = jnp.dot(hi_ref[...], back, preferred_element_type=jnp.float32)
    value = value + jnp.dot(lo_ref[...], back, preferred_element_type=jnp.float32)
    out_ref[...] = value.astype(out_ref.dtype)


def combine(high, low, back):
    return pl.pallas_call(
        combine_kernel,
        out_shape=jax.ShapeDtypeStruct((high.shape[0], back.shape[1]), jnp.bfloat16),
        name="combine",
    )(high, low, back)


def exchange(rows, n_tok):
    blocks = rows.reshape(n_tok, rows.shape[0] // n_tok, rows.shape[1])
    return lax.all_to_all(blocks, "tok", split_axis=0, concat_axis=0, tiled=True).reshape(rows.shape)


def send(value, to):
    pairs = []
    for i in range(CHIPS * CORES):
        chip, core = to(i // CORES, i % CORES)
        pairs.append((i, chip % CHIPS * CORES + core))
    return lax.ppermute(value, "tp", pairs)


def from_near(value):
    return send(value, lambda chip, core: (chip + 1 - 2 * core, core))


def to_near(value):
    return send(value, lambda chip, core: (chip - 1 + 2 * core, core))


def to_near_other(value):
    return send(value, lambda chip, core: (chip - 1 + 2 * core, 1 - core))


def to_sibling(value):
    return send(value, lambda chip, core: (chip, 1 - core))


def block_order(chip, core):
    near = chip - 1 + 2 * core
    chips = jnp.stack([chip, near, near, chip + 2]) & (CHIPS - 1)
    return chips * CORES + jnp.stack([core, core, 1 - core, core])


def expert(own, weights):
    place = lax.axis_index("tp").astype(jnp.int32)
    chip, core = place >> 1, place & 1
    keep, give = pack(jnp.concatenate([block_order(chip, core), block_order(chip, 1 - core)]), weights)
    sib = to_sibling(give)
    half = own.shape[0] // 2
    same_low, same_high = from_near(own[:half]), from_near(own[half:])
    same_low, later = lax.optimization_barrier((same_low, own))
    other = to_near_other(later)
    opposite_low, opposite_high = from_near(same_low), from_near(same_high)
    mine = first(own, same_low, same_high, keep, sib)
    mine = second(other, opposite_low, opposite_high, keep, sib, mine)
    theirs = to_sibling(mine)
    grads_value, for_opposite, for_other = grads(mine, theirs, keep, sib)
    passing, for_other = lax.optimization_barrier((to_near(for_opposite), for_other))
    from_other = to_near_other(for_other)
    from_far = to_near(add(grads_value, keep, sib, (passing,), 1))
    return add(grads_value, keep, sib, (from_far, from_other), 0)


def shards(activations, out_grad, routes, gate_vals, w_gate, w_up, w_down):
    n_tok = lax.axis_size("tok")
    tok_dev, top_k = routes.shape
    capacity = max(2, 2 * tok_dev * top_k // n_tok)
    sent = dispatch(routes, activations, out_grad, n_tok, capacity)
    weights, sent, gate_vals = lax.optimization_barrier(((w_gate[0], w_up[0], w_down[0]), sent, gate_vals))
    high, low = mixer(routes, gate_vals, n_tok, capacity)
    own, high, low = lax.optimization_barrier((exchange(sent, n_tok), high, low))
    expert_sum = expert(own, weights)
    return combine(high, low, exchange(expert_sum, n_tok))


def solution(mesh):
    placed = (
        P("tok", "tp"),
        P("tok", "tp"),
        P("tok", None),
        P("tok", None),
        P("tok", "tp", None),
        P("tok", "tp", None),
        P("tok", "tp", None),
    )
    return jax.shard_map(
        shards, mesh=mesh, in_specs=placed, out_specs=P("tok", "tp"), check_vma=False
    )
```

```python
import functools

import jax
import jax.numpy as jnp
from jax import lax
from jax.experimental import pallas as pl
from jax.experimental.pallas import tpu as pltpu
from jax.sharding import PartitionSpec as P

CHIPS = 4
CORES = 2
CONTRACT_LAST = (((1,), (1,)), ((), ()))
BIG = pltpu.CompilerParams(vmem_limit_bytes=40 * 1024 * 1024)


def places(routes_ref, values, n_tok, capacity):
    top_k, tok_dev = routes_ref.shape
    expert = lax.broadcasted_iota(jnp.int32, (n_tok, tok_dev), 0)
    named = jnp.zeros((n_tok, tok_dev), jnp.float32)
    weight = jnp.zeros((n_tok, tok_dev), jnp.float32)
    for k in range(top_k):
        hit = routes_ref[k : k + 1, :] == expert
        named = named + jnp.where(hit, 1.0, 0.0)
        weight = weight + jnp.where(hit, values[k], 0.0)
    earlier = lax.broadcasted_iota(jnp.int32, (tok_dev, tok_dev), 0)
    later = lax.broadcasted_iota(jnp.int32, (tok_dev, tok_dev), 1)
    ahead = jnp.where(earlier < later, 1.0, 0.0).astype(jnp.bfloat16)
    before = jnp.dot(named.astype(jnp.bfloat16), ahead, preferred_element_type=jnp.float32)
    before = jnp.where(named > 0.0, before, -1.0)
    slot = lax.broadcasted_iota(jnp.int32, (n_tok, capacity, tok_dev), 1).astype(jnp.float32)
    placed = jnp.where(before[:, None, :] == slot, weight[:, None, :], 0.0)
    return placed.reshape(n_tok * capacity, tok_dev)


def dispatch_kernel(n_tok, capacity, routes_ref, x_ref, g_ref, send_ref):
    width = x_ref.shape[1]
    placed = places(routes_ref, (1.0,) * routes_ref.shape[0], n_tok, capacity).astype(jnp.bfloat16)
    send_ref[:, :width] = jnp.dot(placed, x_ref[...], preferred_element_type=jnp.float32).astype(send_ref.dtype)
    send_ref[:, width:] = jnp.dot(placed, g_ref[...], preferred_element_type=jnp.float32).astype(send_ref.dtype)


def dispatch(routes, activations, out_grad, n_tok, capacity):
    width = activations.shape[1]
    return pl.pallas_call(
        functools.partial(dispatch_kernel, n_tok, capacity),
        out_shape=jax.ShapeDtypeStruct((n_tok * capacity, 2 * width), activations.dtype),
        name="dispatch",
    )(routes.T, activations, out_grad)


def mixer_kernel(n_tok, capacity, routes_ref, gates_ref, hi_ref, lo_ref):
    gates = [gates_ref[k : k + 1, :] for k in range(gates_ref.shape[0])]
    scaled = places(routes_ref, gates, n_tok, capacity).T
    high = scaled.astype(jnp.bfloat16)
    hi_ref[...] = high
    lo_ref[...] = (scaled - high.astype(jnp.float32)).astype(jnp.bfloat16)


def mixer(routes, gate_vals, n_tok, capacity):
    part = jax.ShapeDtypeStruct((routes.shape[0], n_tok * capacity), jnp.bfloat16)
    return pl.pallas_call(
        functools.partial(mixer_kernel, n_tok, capacity),
        out_shape=(part, part),
        name="mixer",
    )(routes.T, gate_vals.T)


def pack_kernel(blocks_ref, *refs):
    keep_ref, give_ref = refs[6:]
    hidden = refs[0].shape[0]
    for n in range(3):
        keep_ref[0, n * hidden : (n + 1) * hidden, :] = refs[n][...]
        give_ref[0, n * hidden : (n + 1) * hidden, :] = refs[3 + n][...]


def pack(blocks, weights):
    hidden, width = weights[0].shape
    block = width // (CHIPS * CORES)
    packed = jax.ShapeDtypeStruct((CHIPS, 3 * hidden, block), weights[0].dtype)
    keep = pl.BlockSpec((hidden, block), lambda i, blocks_ref: (0, blocks_ref[i]))
    give = pl.BlockSpec((hidden, block), lambda i, blocks_ref: (0, blocks_ref[i + CHIPS]))
    out = pl.BlockSpec((1, 3 * hidden, block), lambda i, blocks_ref: (i, 0, 0))
    return pl.pallas_call(
        pack_kernel,
        grid_spec=pltpu.PrefetchScalarGridSpec(
            num_scalar_prefetch=1,
            grid=(CHIPS,),
            in_specs=[keep] * 3 + [give] * 3,
            out_specs=[out, out],
        ),
        out_shape=(packed, packed),
        name="pack",
    )(blocks, *weights, *weights)


def products(weight, rows):
    block = weight.shape[1]
    split = weight.shape[0] // 3 * 2
    wide = lax.dot_general(weight[:split], rows[:, :block], CONTRACT_LAST, preferred_element_type=jnp.float32)
    narrow = lax.dot_general(weight[split:], rows[:, block:], CONTRACT_LAST, preferred_element_type=jnp.float32)
    return wide, narrow, split


def first_kernel(own_ref, same_low_ref, same_high_ref, keep_ref, sib_ref, out_ref):
    def store(same_ref):
        for n, weights in enumerate((keep_ref, sib_ref)):
            wide, narrow, split = products(weights[0], own_ref[...])
            same_wide, same_narrow, _ = products(weights[1], same_ref[...])
            out_ref[n, :split, :] = wide + same_wide
            out_ref[n, split:, :] = narrow + same_narrow

    @pl.when(pl.program_id(0) == 0)
    def _():
        store(same_low_ref)

    @pl.when(pl.program_id(0) == 1)
    def _():
        store(same_high_ref)


def first(own, same_low, same_high, keep, sib):
    rows, width = own.shape
    _, depth, block = keep.shape
    half = rows // 2
    whole = pl.BlockSpec((half, width), lambda i: (0, 0))
    weights = pl.BlockSpec((2, depth, block), lambda i: (0, 0, 0))
    return pl.pallas_call(
        first_kernel,
        grid=(2,),
        in_specs=[pl.BlockSpec((half, width), lambda i: (i, 0)), whole, whole, weights, weights],
        out_specs=pl.BlockSpec((CORES, depth, half), lambda i: (0, 0, i)),
        out_shape=jax.ShapeDtypeStruct((CORES, depth, rows), jnp.float32),
        compiler_params=BIG,
        name="first",
    )(own, same_low, same_high, keep, sib)


def second_kernel(other_ref, low_ref, high_ref, keep_ref, sib_ref, sum_ref, out_ref):
    def add(rows_ref):
        for n, weights in enumerate((keep_ref, sib_ref)):
            wide, narrow, split = products(weights[0], other_ref[...])
            far_wide, far_narrow, _ = products(weights[1], rows_ref[...])
            out_ref[n, :split, :] = sum_ref[n, :split, :] + (wide + far_wide)
            out_ref[n, split:, :] = sum_ref[n, split:, :] + (narrow + far_narrow)

    @pl.when(pl.program_id(0) == 0)
    def _():
        add(low_ref)

    @pl.when(pl.program_id(0) == 1)
    def _():
        add(high_ref)


def second(other, low, high, keep, sib, sums):
    half, width = low.shape
    _, depth, block = keep.shape
    whole = pl.BlockSpec((half, width), lambda i: (0, 0))
    weights = pl.BlockSpec((2, depth, block), lambda i: (1, 0, 0))
    by_half = pl.BlockSpec((CORES, depth, half), lambda i: (0, 0, i))
    return pl.pallas_call(
        second_kernel,
        grid=(2,),
        in_specs=[pl.BlockSpec((half, width), lambda i: (i, 0)), whole, whole, weights, weights, by_half],
        out_specs=by_half,
        out_shape=jax.ShapeDtypeStruct(sums.shape, sums.dtype),
        compiler_params=BIG,
        name="second",
    )(other, low, high, keep, sib, sums)


def chip_sum(grads, keep, sib):
    depth = grads.shape[1]
    return jnp.dot(grads[0].T, keep[:depth, :], preferred_element_type=jnp.float32) + jnp.dot(
        grads[1].T, sib[:depth, :], preferred_element_type=jnp.float32
    )


def grads_kernel(mine_ref, theirs_ref, keep_ref, sib_ref, grads_ref, low_ref, high_ref, other_ref):
    hidden = mine_ref.shape[1] // 3
    for n in range(CORES):
        gate_pre = mine_ref[n, :hidden, :] + theirs_ref[1 - n, :hidden, :]
        up_pre = mine_ref[n, hidden : 2 * hidden, :] + theirs_ref[1 - n, hidden : 2 * hidden, :]
        hidden_grad = mine_ref[n, 2 * hidden :, :] + theirs_ref[1 - n, 2 * hidden :, :]
        sigma = 1.0 / (1.0 + jnp.exp(-gate_pre))
        slope = sigma * (1.0 + gate_pre * (1.0 - sigma))
        grads_ref[n, :hidden, :] = (hidden_grad * up_pre * slope).astype(grads_ref.dtype)
        grads_ref[n, hidden:, :] = (hidden_grad * (gate_pre * sigma)).astype(grads_ref.dtype)
    other_ref[...] = chip_sum(grads_ref[...], keep_ref[0], sib_ref[0]).astype(other_ref.dtype)
    value = chip_sum(grads_ref[...], keep_ref[1], sib_ref[1]).astype(low_ref.dtype)

    @pl.when(pl.program_id(0) == 0)
    def _():
        low_ref[...] = value

    @pl.when(pl.program_id(0) == 1)
    def _():
        high_ref[...] = value


def grads(mine, theirs, keep, sib):
    _, depth, rows = mine.shape
    block = keep.shape[2]
    half = rows // 2
    wide = depth // 3 * 2
    by_half = pl.BlockSpec((CORES, depth, half), lambda i: (0, 0, i))
    weights = pl.BlockSpec((2, depth, block), lambda i: (1, 0, 0))
    whole = pl.BlockSpec((half, block), lambda i: (0, 0))
    part = jax.ShapeDtypeStruct((half, block), jnp.bfloat16)
    return pl.pallas_call(
        grads_kernel,
        grid=(2,),
        in_specs=[by_half] * 2 + [weights] * 2,
        out_specs=[
            pl.BlockSpec((CORES, wide, half), lambda i: (0, 0, i)),
            whole,
            whole,
            pl.BlockSpec((half, block), lambda i: (i, 0)),
        ],
        out_shape=(
            jax.ShapeDtypeStruct((CORES, wide, rows), jnp.bfloat16),
            part,
            part,
            jax.ShapeDtypeStruct((rows, block), jnp.bfloat16),
        ),
        compiler_params=BIG,
        name="grads",
    )(mine, theirs, keep, sib)


def near_kernel(grads_ref, keep_ref, sib_ref, got_ref, out_ref):
    value = chip_sum(grads_ref[...], keep_ref[0], sib_ref[0]) + got_ref[...].astype(jnp.float32)
    out_ref[...] = value.astype(out_ref.dtype)


def near(grads_value, keep, sib, got, part):
    _, wide, _ = grads_value.shape
    _, depth, block = keep.shape
    half = got.shape[0]
    weights = pl.BlockSpec((1, depth, block), lambda i: (1, 0, 0))
    whole = pl.BlockSpec((half, block), lambda i: (0, 0))
    return pl.pallas_call(
        near_kernel,
        grid=(1,),
        in_specs=[pl.BlockSpec((CORES, wide, half), lambda i: (0, 0, part)), weights, weights, whole],
        out_specs=whole,
        out_shape=jax.ShapeDtypeStruct(got.shape, jnp.bfloat16),
        compiler_params=BIG,
        name="near",
    )(grads_value, keep, sib, got)


def total_kernel(grads_ref, keep_ref, sib_ref, low_ref, high_ref, other_ref, out_ref):
    value = chip_sum(grads_ref[...], keep_ref[0], sib_ref[0]) + other_ref[...].astype(jnp.float32)

    @pl.when(pl.program_id(0) == 0)
    def _():
        out_ref[...] = (value + low_ref[...].astype(jnp.float32)).astype(out_ref.dtype)

    @pl.when(pl.program_id(0) == 1)
    def _():
        out_ref[...] = (value + high_ref[...].astype(jnp.float32)).astype(out_ref.dtype)


def total(grads_value, keep, sib, low, high, other):
    _, wide, rows = grads_value.shape
    _, depth, block = keep.shape
    half = rows // 2
    weights = pl.BlockSpec((1, depth, block), lambda i: (0, 0, 0))
    whole = pl.BlockSpec((half, block), lambda i: (0, 0))
    by_half = pl.BlockSpec((half, block), lambda i: (i, 0))
    return pl.pallas_call(
        total_kernel,
        grid=(2,),
        in_specs=[pl.BlockSpec((CORES, wide, half), lambda i: (0, 0, i)), weights, weights, whole, whole, by_half],
        out_specs=by_half,
        out_shape=jax.ShapeDtypeStruct((rows, block), jnp.bfloat16),
        compiler_params=BIG,
        name="total",
    )(grads_value, keep, sib, low, high, other)


def combine_kernel(hi_ref, lo_ref, back_ref, out_ref):
    back = back_ref[...]
    value = jnp.dot(hi_ref[...], back, preferred_element_type=jnp.float32)
    value = value + jnp.dot(lo_ref[...], back, preferred_element_type=jnp.float32)
    out_ref[...] = value.astype(out_ref.dtype)


def combine(high, low, back):
    return pl.pallas_call(
        combine_kernel,
        out_shape=jax.ShapeDtypeStruct((high.shape[0], back.shape[1]), jnp.bfloat16),
        name="combine",
    )(high, low, back)


def exchange(rows, n_tok):
    blocks = rows.reshape(n_tok, rows.shape[0] // n_tok, rows.shape[1])
    return lax.all_to_all(blocks, "tok", split_axis=0, concat_axis=0, tiled=True).reshape(rows.shape)


def send(value, to):
    pairs = []
    for i in range(CHIPS * CORES):
        chip, core = to(i // CORES, i % CORES)
        pairs.append((i, chip % CHIPS * CORES + core))
    return lax.ppermute(value, "tp", pairs)


def from_near(value):
    return send(value, lambda chip, core: (chip + 1 - 2 * core, core))


def to_near(value):
    return send(value, lambda chip, core: (chip - 1 + 2 * core, core))


def to_near_other(value):
    return send(value, lambda chip, core: (chip - 1 + 2 * core, 1 - core))


def to_sibling(value):
    return send(value, lambda chip, core: (chip, 1 - core))


def block_order(chip, core):
    near = chip - 1 + 2 * core
    chips = jnp.stack([chip, near, near, chip + 2]) & (CHIPS - 1)
    return chips * CORES + jnp.stack([core, core, 1 - core, core])


def expert(own, weights):
    place = lax.axis_index("tp").astype(jnp.int32)
    chip, core = place >> 1, place & 1
    keep, give = pack(jnp.concatenate([block_order(chip, core), block_order(chip, 1 - core)]), weights)
    sib = to_sibling(give)
    half = own.shape[0] // 2
    same_low, same_high = from_near(own[:half]), from_near(own[half:])
    same_low, later = lax.optimization_barrier((same_low, own))
    other = to_near_other(later)
    opposite_low, opposite_high = from_near(same_low), from_near(same_high)
    mine = first(own, same_low, same_high, keep, sib)
    mine = second(other, opposite_low, opposite_high, keep, sib, mine)
    theirs = to_sibling(mine)
    grads_value, part_low, part_high, for_other = grads(mine, theirs, keep, sib)
    passing_low, passing_high = to_near(part_low), to_near(part_high)
    from_other = to_near_other(for_other)
    from_low = to_near(near(grads_value, keep, sib, passing_low, 0))
    from_high = to_near(near(grads_value, keep, sib, passing_high, 1))
    return total(grads_value, keep, sib, from_low, from_high, from_other)


def shards(activations, out_grad, routes, gate_vals, w_gate, w_up, w_down):
    n_tok = lax.axis_size("tok")
    tok_dev, top_k = routes.shape
    capacity = max(2, 2 * tok_dev * top_k // n_tok)
    sent = dispatch(routes, activations, out_grad, n_tok, capacity)
    weights, sent, gate_vals = lax.optimization_barrier(((w_gate[0], w_up[0], w_down[0]), sent, gate_vals))
    high, low = mixer(routes, gate_vals, n_tok, capacity)
    own, high, low = lax.optimization_barrier((exchange(sent, n_tok), high, low))
    expert_sum = expert(own, weights)
    return combine(high, low, exchange(expert_sum, n_tok))


def solution(mesh):
    placed = (
        P("tok", "tp"),
        P("tok", "tp"),
        P("tok", None),
        P("tok", None),
        P("tok", "tp", None),
        P("tok", "tp", None),
        P("tok", "tp", None),
    )
    return jax.shard_map(
        shards, mesh=mesh, in_specs=placed, out_specs=P("tok", "tp"), check_vma=False
    )
```

```python
import functools

import jax
import jax.numpy as jnp
from jax import lax
from jax.experimental import pallas as pl
from jax.experimental.pallas import tpu as pltpu
from jax.sharding import PartitionSpec as P

CHIPS = 4
CORES = 2
CONTRACT_LAST = (((1,), (1,)), ((), ()))
BIG = pltpu.CompilerParams(vmem_limit_bytes=40 * 1024 * 1024)


def places(routes_ref, values, n_tok, capacity):
    top_k, tok_dev = routes_ref.shape
    expert = lax.broadcasted_iota(jnp.int32, (n_tok, tok_dev), 0)
    named = jnp.zeros((n_tok, tok_dev), jnp.float32)
    weight = jnp.zeros((n_tok, tok_dev), jnp.float32)
    for k in range(top_k):
        hit = routes_ref[k : k + 1, :] == expert
        named = named + jnp.where(hit, 1.0, 0.0)
        weight = weight + jnp.where(hit, values[k], 0.0)
    earlier = lax.broadcasted_iota(jnp.int32, (tok_dev, tok_dev), 0)
    later = lax.broadcasted_iota(jnp.int32, (tok_dev, tok_dev), 1)
    ahead = jnp.where(earlier < later, 1.0, 0.0).astype(jnp.bfloat16)
    before = jnp.dot(named.astype(jnp.bfloat16), ahead, preferred_element_type=jnp.float32)
    before = jnp.where(named > 0.0, before, -1.0)
    slot = lax.broadcasted_iota(jnp.int32, (n_tok, capacity, tok_dev), 1).astype(jnp.float32)
    placed = jnp.where(before[:, None, :] == slot, weight[:, None, :], 0.0)
    return placed.reshape(n_tok * capacity, tok_dev)


def dispatch_kernel(n_tok, capacity, routes_ref, x_ref, g_ref, send_ref):
    width = x_ref.shape[1]
    placed = places(routes_ref, (1.0,) * routes_ref.shape[0], n_tok, capacity).astype(jnp.bfloat16)
    send_ref[:, :width] = jnp.dot(placed, x_ref[...], preferred_element_type=jnp.float32).astype(send_ref.dtype)
    send_ref[:, width:] = jnp.dot(placed, g_ref[...], preferred_element_type=jnp.float32).astype(send_ref.dtype)


def dispatch(routes, activations, out_grad, n_tok, capacity):
    width = activations.shape[1]
    return pl.pallas_call(
        functools.partial(dispatch_kernel, n_tok, capacity),
        out_shape=jax.ShapeDtypeStruct((n_tok * capacity, 2 * width), activations.dtype),
        name="dispatch",
    )(routes.T, activations, out_grad)


def mixer_kernel(n_tok, capacity, routes_ref, gates_ref, hi_ref, lo_ref):
    gates = [gates_ref[k : k + 1, :] for k in range(gates_ref.shape[0])]
    scaled = places(routes_ref, gates, n_tok, capacity).T
    high = scaled.astype(jnp.bfloat16)
    hi_ref[...] = high
    lo_ref[...] = (scaled - high.astype(jnp.float32)).astype(jnp.bfloat16)


def mixer(routes, gate_vals, n_tok, capacity):
    part = jax.ShapeDtypeStruct((routes.shape[0], n_tok * capacity), jnp.bfloat16)
    return pl.pallas_call(
        functools.partial(mixer_kernel, n_tok, capacity),
        out_shape=(part, part),
        name="mixer",
    )(routes.T, gate_vals.T)


def pack_kernel(blocks_ref, *refs):
    keep_ref, give_ref = refs[6:]
    hidden = refs[0].shape[0]
    for n in range(3):
        keep_ref[0, n * hidden : (n + 1) * hidden, :] = refs[n][...]
        give_ref[0, n * hidden : (n + 1) * hidden, :] = refs[3 + n][...]


def pack(blocks, weights):
    hidden, width = weights[0].shape
    block = width // (CHIPS * CORES)
    packed = jax.ShapeDtypeStruct((CHIPS, 3 * hidden, block), weights[0].dtype)
    keep = pl.BlockSpec((hidden, block), lambda i, blocks_ref: (0, blocks_ref[i]))
    give = pl.BlockSpec((hidden, block), lambda i, blocks_ref: (0, blocks_ref[i + CHIPS]))
    out = pl.BlockSpec((1, 3 * hidden, block), lambda i, blocks_ref: (i, 0, 0))
    return pl.pallas_call(
        pack_kernel,
        grid_spec=pltpu.PrefetchScalarGridSpec(
            num_scalar_prefetch=1,
            grid=(CHIPS,),
            in_specs=[keep] * 3 + [give] * 3,
            out_specs=[out, out],
        ),
        out_shape=(packed, packed),
        name="pack",
    )(blocks, *weights, *weights)


def products(weight, rows):
    block = weight.shape[1]
    split = weight.shape[0] // 3 * 2
    wide = lax.dot_general(weight[:split], rows[:, :block], CONTRACT_LAST, preferred_element_type=jnp.float32)
    narrow = lax.dot_general(weight[split:], rows[:, block:], CONTRACT_LAST, preferred_element_type=jnp.float32)
    return wide, narrow, split


def first_kernel(own_ref, same_low_ref, same_high_ref, keep_ref, sib_ref, out_ref):
    def store(same_ref):
        for n, weights in enumerate((keep_ref, sib_ref)):
            wide, narrow, split = products(weights[0], own_ref[...])
            same_wide, same_narrow, _ = products(weights[1], same_ref[...])
            out_ref[n, :split, :] = wide + same_wide
            out_ref[n, split:, :] = narrow + same_narrow

    @pl.when(pl.program_id(0) == 0)
    def _():
        store(same_low_ref)

    @pl.when(pl.program_id(0) == 1)
    def _():
        store(same_high_ref)


def first(own, same_low, same_high, keep, sib):
    rows, width = own.shape
    _, depth, block = keep.shape
    half = rows // 2
    whole = pl.BlockSpec((half, width), lambda i: (0, 0))
    weights = pl.BlockSpec((2, depth, block), lambda i: (0, 0, 0))
    return pl.pallas_call(
        first_kernel,
        grid=(2,),
        in_specs=[pl.BlockSpec((half, width), lambda i: (i, 0)), whole, whole, weights, weights],
        out_specs=pl.BlockSpec((CORES, depth, half), lambda i: (0, 0, i)),
        out_shape=jax.ShapeDtypeStruct((CORES, depth, rows), jnp.float32),
        compiler_params=BIG,
        name="first",
    )(own, same_low, same_high, keep, sib)


def second_kernel(other_low_ref, other_high_ref, low_ref, high_ref, keep_ref, sib_ref, sum_ref, out_ref):
    def add(other_ref, rows_ref):
        for n, weights in enumerate((keep_ref, sib_ref)):
            wide, narrow, split = products(weights[0], other_ref[...])
            far_wide, far_narrow, _ = products(weights[1], rows_ref[...])
            out_ref[n, :split, :] = sum_ref[n, :split, :] + (wide + far_wide)
            out_ref[n, split:, :] = sum_ref[n, split:, :] + (narrow + far_narrow)

    @pl.when(pl.program_id(0) == 0)
    def _():
        add(other_low_ref, low_ref)

    @pl.when(pl.program_id(0) == 1)
    def _():
        add(other_high_ref, high_ref)


def second(other, opposite, keep, sib, sums):
    half, width = other[0].shape
    _, depth, block = keep.shape
    whole = pl.BlockSpec((half, width), lambda i: (0, 0))
    weights = pl.BlockSpec((2, depth, block), lambda i: (1, 0, 0))
    by_half = pl.BlockSpec((CORES, depth, half), lambda i: (0, 0, i))
    return pl.pallas_call(
        second_kernel,
        grid=(2,),
        in_specs=[whole] * 4 + [weights, weights, by_half],
        out_specs=by_half,
        out_shape=jax.ShapeDtypeStruct(sums.shape, sums.dtype),
        compiler_params=BIG,
        name="second",
    )(*other, *opposite, keep, sib, sums)


def chip_sum(grads, keep, sib):
    depth = grads.shape[1]
    return jnp.dot(grads[0].T, keep[:depth, :], preferred_element_type=jnp.float32) + jnp.dot(
        grads[1].T, sib[:depth, :], preferred_element_type=jnp.float32
    )


def grads_kernel(mine_ref, theirs_ref, keep_ref, sib_ref, grads_ref, low_ref, high_ref, other_ref):
    hidden = mine_ref.shape[1] // 3
    for n in range(CORES):
        gate_pre = mine_ref[n, :hidden, :] + theirs_ref[1 - n, :hidden, :]
        up_pre = mine_ref[n, hidden : 2 * hidden, :] + theirs_ref[1 - n, hidden : 2 * hidden, :]
        hidden_grad = mine_ref[n, 2 * hidden :, :] + theirs_ref[1 - n, 2 * hidden :, :]
        sigma = 1.0 / (1.0 + jnp.exp(-gate_pre))
        slope = sigma * (1.0 + gate_pre * (1.0 - sigma))
        grads_ref[n, :hidden, :] = (hidden_grad * up_pre * slope).astype(grads_ref.dtype)
        grads_ref[n, hidden:, :] = (hidden_grad * (gate_pre * sigma)).astype(grads_ref.dtype)
    other_ref[...] = chip_sum(grads_ref[...], keep_ref[0], sib_ref[0]).astype(other_ref.dtype)
    value = chip_sum(grads_ref[...], keep_ref[1], sib_ref[1]).astype(low_ref.dtype)

    @pl.when(pl.program_id(0) == 0)
    def _():
        low_ref[...] = value

    @pl.when(pl.program_id(0) == 1)
    def _():
        high_ref[...] = value


def grads(mine, theirs, keep, sib):
    _, depth, rows = mine.shape
    block = keep.shape[2]
    half = rows // 2
    wide = depth // 3 * 2
    by_half = pl.BlockSpec((CORES, depth, half), lambda i: (0, 0, i))
    weights = pl.BlockSpec((2, depth, block), lambda i: (1, 0, 0))
    whole = pl.BlockSpec((half, block), lambda i: (0, 0))
    part = jax.ShapeDtypeStruct((half, block), jnp.bfloat16)
    return pl.pallas_call(
        grads_kernel,
        grid=(2,),
        in_specs=[by_half] * 2 + [weights] * 2,
        out_specs=[
            pl.BlockSpec((CORES, wide, half), lambda i: (0, 0, i)),
            whole,
            whole,
            pl.BlockSpec((half, block), lambda i: (i, 0)),
        ],
        out_shape=(
            jax.ShapeDtypeStruct((CORES, wide, rows), jnp.bfloat16),
            part,
            part,
            jax.ShapeDtypeStruct((rows, block), jnp.bfloat16),
        ),
        compiler_params=BIG,
        name="grads",
    )(mine, theirs, keep, sib)


def near_kernel(grads_ref, keep_ref, sib_ref, got_ref, out_ref):
    value = chip_sum(grads_ref[...], keep_ref[0], sib_ref[0]) + got_ref[...].astype(jnp.float32)
    out_ref[...] = value.astype(out_ref.dtype)


def near(grads_value, keep, sib, got, part):
    _, wide, _ = grads_value.shape
    _, depth, block = keep.shape
    half = got.shape[0]
    weights = pl.BlockSpec((1, depth, block), lambda i: (1, 0, 0))
    whole = pl.BlockSpec((half, block), lambda i: (0, 0))
    return pl.pallas_call(
        near_kernel,
        grid=(1,),
        in_specs=[pl.BlockSpec((CORES, wide, half), lambda i: (0, 0, part)), weights, weights, whole],
        out_specs=whole,
        out_shape=jax.ShapeDtypeStruct(got.shape, jnp.bfloat16),
        compiler_params=BIG,
        name="near",
    )(grads_value, keep, sib, got)


def total_kernel(grads_ref, keep_ref, sib_ref, low_ref, high_ref, other_ref, out_ref):
    value = chip_sum(grads_ref[...], keep_ref[0], sib_ref[0]) + other_ref[...].astype(jnp.float32)

    @pl.when(pl.program_id(0) == 0)
    def _():
        out_ref[...] = (value + low_ref[...].astype(jnp.float32)).astype(out_ref.dtype)

    @pl.when(pl.program_id(0) == 1)
    def _():
        out_ref[...] = (value + high_ref[...].astype(jnp.float32)).astype(out_ref.dtype)


def total(grads_value, keep, sib, low, high, other):
    _, wide, rows = grads_value.shape
    _, depth, block = keep.shape
    half = rows // 2
    weights = pl.BlockSpec((1, depth, block), lambda i: (0, 0, 0))
    whole = pl.BlockSpec((half, block), lambda i: (0, 0))
    by_half = pl.BlockSpec((half, block), lambda i: (i, 0))
    return pl.pallas_call(
        total_kernel,
        grid=(2,),
        in_specs=[pl.BlockSpec((CORES, wide, half), lambda i: (0, 0, i)), weights, weights, whole, whole, by_half],
        out_specs=by_half,
        out_shape=jax.ShapeDtypeStruct((rows, block), jnp.bfloat16),
        compiler_params=BIG,
        name="total",
    )(grads_value, keep, sib, low, high, other)


def combine_kernel(hi_ref, lo_ref, back_ref, out_ref):
    back = back_ref[...]
    value = jnp.dot(hi_ref[...], back, preferred_element_type=jnp.float32)
    value = value + jnp.dot(lo_ref[...], back, preferred_element_type=jnp.float32)
    out_ref[...] = value.astype(out_ref.dtype)


def combine(high, low, back):
    return pl.pallas_call(
        combine_kernel,
        out_shape=jax.ShapeDtypeStruct((high.shape[0], back.shape[1]), jnp.bfloat16),
        name="combine",
    )(high, low, back)


def exchange(rows, n_tok):
    blocks = rows.reshape(n_tok, rows.shape[0] // n_tok, rows.shape[1])
    return lax.all_to_all(blocks, "tok", split_axis=0, concat_axis=0, tiled=True).reshape(rows.shape)


def send(value, to):
    pairs = []
    for i in range(CHIPS * CORES):
        chip, core = to(i // CORES, i % CORES)
        pairs.append((i, chip % CHIPS * CORES + core))
    return lax.ppermute(value, "tp", pairs)


def from_near(value):
    return send(value, lambda chip, core: (chip + 1 - 2 * core, core))


def to_near(value):
    return send(value, lambda chip, core: (chip - 1 + 2 * core, core))


def to_near_other(value):
    return send(value, lambda chip, core: (chip - 1 + 2 * core, 1 - core))


def to_sibling(value):
    return send(value, lambda chip, core: (chip, 1 - core))


def block_order(chip, core):
    near = chip - 1 + 2 * core
    chips = jnp.stack([chip, near, near, chip + 2]) & (CHIPS - 1)
    return chips * CORES + jnp.stack([core, core, 1 - core, core])


def expert(own, weights):
    place = lax.axis_index("tp").astype(jnp.int32)
    chip, core = place >> 1, place & 1
    keep, give = pack(jnp.concatenate([block_order(chip, core), block_order(chip, 1 - core)]), weights)
    sib = to_sibling(give)
    half = own.shape[0] // 2
    halves = (own[:half], own[half:])
    same = [from_near(rows) for rows in halves]
    other = [to_near_other(rows) for rows in halves]
    opposite = [from_near(rows) for rows in same]
    mine = first(own, *same, keep, sib)
    mine = second(other, opposite, keep, sib, mine)
    theirs = to_sibling(mine)
    grads_value, part_low, part_high, for_other = grads(mine, theirs, keep, sib)
    passing_low, passing_high = to_near(part_low), to_near(part_high)
    from_other = to_near_other(for_other)
    from_low = to_near(near(grads_value, keep, sib, passing_low, 0))
    from_high = to_near(near(grads_value, keep, sib, passing_high, 1))
    return total(grads_value, keep, sib, from_low, from_high, from_other)


def shards(activations, out_grad, routes, gate_vals, w_gate, w_up, w_down):
    n_tok = lax.axis_size("tok")
    tok_dev, top_k = routes.shape
    capacity = max(2, 2 * tok_dev * top_k // n_tok)
    sent = dispatch(routes, activations, out_grad, n_tok, capacity)
    weights, sent, gate_vals = lax.optimization_barrier(((w_gate[0], w_up[0], w_down[0]), sent, gate_vals))
    high, low = mixer(routes, gate_vals, n_tok, capacity)
    own, high, low = lax.optimization_barrier((exchange(sent, n_tok), high, low))
    expert_sum = expert(own, weights)
    return combine(high, low, exchange(expert_sum, n_tok))


def solution(mesh):
    placed = (
        P("tok", "tp"),
        P("tok", "tp"),
        P("tok", None),
        P("tok", None),
        P("tok", "tp", None),
        P("tok", "tp", None),
        P("tok", "tp", None),
    )
    return jax.shard_map(
        shards, mesh=mesh, in_specs=placed, out_specs=P("tok", "tp"), check_vma=False
    )
```

```python
import functools

import jax
import jax.numpy as jnp
from jax import lax
from jax.experimental import pallas as pl
from jax.experimental.pallas import tpu as pltpu
from jax.sharding import PartitionSpec as P

CHIPS = 4
CORES = 2
CONTRACT_LAST = (((1,), (1,)), ((), ()))
BIG = pltpu.CompilerParams(vmem_limit_bytes=40 * 1024 * 1024)


def places(routes_ref, values, n_tok, capacity):
    top_k, tok_dev = routes_ref.shape
    expert = lax.broadcasted_iota(jnp.int32, (n_tok, tok_dev), 0)
    named = jnp.zeros((n_tok, tok_dev), jnp.float32)
    weight = jnp.zeros((n_tok, tok_dev), jnp.float32)
    for k in range(top_k):
        hit = routes_ref[k : k + 1, :] == expert
        named = named + jnp.where(hit, 1.0, 0.0)
        weight = weight + jnp.where(hit, values[k], 0.0)
    earlier = lax.broadcasted_iota(jnp.int32, (tok_dev, tok_dev), 0)
    later = lax.broadcasted_iota(jnp.int32, (tok_dev, tok_dev), 1)
    ahead = jnp.where(earlier < later, 1.0, 0.0).astype(jnp.bfloat16)
    before = jnp.dot(named.astype(jnp.bfloat16), ahead, preferred_element_type=jnp.float32)
    before = jnp.where(named > 0.0, before, -1.0)
    slot = lax.broadcasted_iota(jnp.int32, (n_tok, capacity, tok_dev), 1).astype(jnp.float32)
    placed = jnp.where(before[:, None, :] == slot, weight[:, None, :], 0.0)
    return placed.reshape(n_tok * capacity, tok_dev)


def dispatch_kernel(n_tok, capacity, routes_ref, x_ref, g_ref, send_ref):
    width = x_ref.shape[1]
    placed = places(routes_ref, (1.0,) * routes_ref.shape[0], n_tok, capacity).astype(jnp.bfloat16)
    send_ref[:, :width] = jnp.dot(placed, x_ref[...], preferred_element_type=jnp.float32).astype(send_ref.dtype)
    send_ref[:, width:] = jnp.dot(placed, g_ref[...], preferred_element_type=jnp.float32).astype(send_ref.dtype)


def dispatch(routes, activations, out_grad, n_tok, capacity):
    width = activations.shape[1]
    return pl.pallas_call(
        functools.partial(dispatch_kernel, n_tok, capacity),
        out_shape=jax.ShapeDtypeStruct((n_tok * capacity, 2 * width), activations.dtype),
        name="dispatch",
    )(routes.T, activations, out_grad)


def mixer_kernel(n_tok, capacity, routes_ref, gates_ref, hi_ref, lo_ref):
    gates = [gates_ref[k : k + 1, :] for k in range(gates_ref.shape[0])]
    scaled = places(routes_ref, gates, n_tok, capacity).T
    high = scaled.astype(jnp.bfloat16)
    hi_ref[...] = high
    lo_ref[...] = (scaled - high.astype(jnp.float32)).astype(jnp.bfloat16)


def mixer(routes, gate_vals, n_tok, capacity):
    part = jax.ShapeDtypeStruct((routes.shape[0], n_tok * capacity), jnp.bfloat16)
    return pl.pallas_call(
        functools.partial(mixer_kernel, n_tok, capacity),
        out_shape=(part, part),
        name="mixer",
    )(routes.T, gate_vals.T)


def pack_kernel(blocks_ref, *refs):
    keep_ref, give_ref = refs[6:]
    hidden = refs[0].shape[0]
    for n in range(3):
        keep_ref[0, n * hidden : (n + 1) * hidden, :] = refs[n][...]
        give_ref[0, n * hidden : (n + 1) * hidden, :] = refs[3 + n][...]


def pack(blocks, weights):
    hidden, width = weights[0].shape
    block = width // (CHIPS * CORES)
    packed = jax.ShapeDtypeStruct((CHIPS, 3 * hidden, block), weights[0].dtype)
    keep = pl.BlockSpec((hidden, block), lambda i, blocks_ref: (0, blocks_ref[i]))
    give = pl.BlockSpec((hidden, block), lambda i, blocks_ref: (0, blocks_ref[i + CHIPS]))
    out = pl.BlockSpec((1, 3 * hidden, block), lambda i, blocks_ref: (i, 0, 0))
    return pl.pallas_call(
        pack_kernel,
        grid_spec=pltpu.PrefetchScalarGridSpec(
            num_scalar_prefetch=1,
            grid=(CHIPS,),
            in_specs=[keep] * 3 + [give] * 3,
            out_specs=[out, out],
        ),
        out_shape=(packed, packed),
        name="pack",
    )(blocks, *weights, *weights)


def products(weight, rows):
    block = weight.shape[1]
    split = weight.shape[0] // 3 * 2
    wide = lax.dot_general(weight[:split], rows[:, :block], CONTRACT_LAST, preferred_element_type=jnp.float32)
    narrow = lax.dot_general(weight[split:], rows[:, block:], CONTRACT_LAST, preferred_element_type=jnp.float32)
    return wide, narrow, split


def first_kernel(own_ref, same_low_ref, same_high_ref, keep_ref, sib_ref, out_ref):
    def store(same_ref):
        for n, weights in enumerate((keep_ref, sib_ref)):
            wide, narrow, split = products(weights[0], own_ref[...])
            same_wide, same_narrow, _ = products(weights[1], same_ref[...])
            out_ref[n, :split, :] = wide + same_wide
            out_ref[n, split:, :] = narrow + same_narrow

    @pl.when(pl.program_id(0) == 0)
    def _():
        store(same_low_ref)

    @pl.when(pl.program_id(0) == 1)
    def _():
        store(same_high_ref)


def first(own, same_low, same_high, keep, sib):
    rows, width = own.shape
    _, depth, block = keep.shape
    half = rows // 2
    whole = pl.BlockSpec((half, width), lambda i: (0, 0))
    weights = pl.BlockSpec((2, depth, block), lambda i: (0, 0, 0))
    return pl.pallas_call(
        first_kernel,
        grid=(2,),
        in_specs=[pl.BlockSpec((half, width), lambda i: (i, 0)), whole, whole, weights, weights],
        out_specs=pl.BlockSpec((CORES, depth, half), lambda i: (0, 0, i)),
        out_shape=jax.ShapeDtypeStruct((CORES, depth, rows), jnp.float32),
        compiler_params=BIG,
        name="first",
    )(own, same_low, same_high, keep, sib)


def second_kernel(other_ref, opposite_ref, keep_ref, sib_ref, sum_ref, out_ref):
    for n, weights in enumerate((keep_ref, sib_ref)):
        wide, narrow, split = products(weights[0], other_ref[...])
        far_wide, far_narrow, _ = products(weights[1], opposite_ref[...])
        out_ref[n, :split, :] = sum_ref[n, :split, :] + (wide + far_wide)
        out_ref[n, split:, :] = sum_ref[n, split:, :] + (narrow + far_narrow)


def second(other, opposite, keep, sib, sums, part):
    half, width = other.shape
    _, depth, block = keep.shape
    whole = pl.BlockSpec((half, width), lambda i: (0, 0))
    weights = pl.BlockSpec((2, depth, block), lambda i: (1, 0, 0))
    return pl.pallas_call(
        second_kernel,
        grid=(1,),
        in_specs=[whole, whole, weights, weights, pl.BlockSpec((CORES, depth, half), lambda i: (0, 0, part))],
        out_specs=pl.BlockSpec((CORES, depth, half), lambda i: (0, 0, 0)),
        out_shape=jax.ShapeDtypeStruct((CORES, depth, half), sums.dtype),
        compiler_params=BIG,
        name="second",
    )(other, opposite, keep, sib, sums)


def chip_sum(grads, keep, sib):
    depth = grads.shape[1]
    return jnp.dot(grads[0].T, keep[:depth, :], preferred_element_type=jnp.float32) + jnp.dot(
        grads[1].T, sib[:depth, :], preferred_element_type=jnp.float32
    )


def grads_kernel(mine_ref, theirs_ref, keep_ref, sib_ref, grads_ref, part_ref):
    hidden = mine_ref.shape[1] // 3
    for n in range(CORES):
        gate_pre = mine_ref[n, :hidden, :] + theirs_ref[1 - n, :hidden, :]
        up_pre = mine_ref[n, hidden : 2 * hidden, :] + theirs_ref[1 - n, hidden : 2 * hidden, :]
        hidden_grad = mine_ref[n, 2 * hidden :, :] + theirs_ref[1 - n, 2 * hidden :, :]
        sigma = 1.0 / (1.0 + jnp.exp(-gate_pre))
        slope = sigma * (1.0 + gate_pre * (1.0 - sigma))
        grads_ref[n, :hidden, :] = (hidden_grad * up_pre * slope).astype(grads_ref.dtype)
        grads_ref[n, hidden:, :] = (hidden_grad * (gate_pre * sigma)).astype(grads_ref.dtype)
    part_ref[...] = chip_sum(grads_ref[...], keep_ref[0], sib_ref[0]).astype(part_ref.dtype)


def grads(mine, theirs, keep, sib):
    _, depth, half = mine.shape
    block = keep.shape[2]
    wide = depth // 3 * 2
    whole = pl.BlockSpec((CORES, depth, half), lambda i: (0, 0, 0))
    weights = pl.BlockSpec((1, depth, block), lambda i: (CHIPS - 1, 0, 0))
    return pl.pallas_call(
        grads_kernel,
        grid=(1,),
        in_specs=[whole, whole, weights, weights],
        out_specs=[pl.BlockSpec((CORES, wide, half), lambda i: (0, 0, 0)), pl.BlockSpec((half, block), lambda i: (0, 0))],
        out_shape=(jax.ShapeDtypeStruct((CORES, wide, half), jnp.bfloat16), jax.ShapeDtypeStruct((half, block), jnp.bfloat16)),
        compiler_params=BIG,
        name="grads",
    )(mine, theirs, keep, sib)


def near_kernel(grads_ref, keep_ref, sib_ref, got_ref, out_ref):
    value = chip_sum(grads_ref[...], keep_ref[0], sib_ref[0]) + got_ref[...].astype(jnp.float32)
    out_ref[...] = value.astype(out_ref.dtype)


def near(grads_value, keep, sib, got):
    _, wide, half = grads_value.shape
    _, depth, block = keep.shape
    weights = pl.BlockSpec((1, depth, block), lambda i: (1, 0, 0))
    whole = pl.BlockSpec((half, block), lambda i: (0, 0))
    return pl.pallas_call(
        near_kernel,
        grid=(1,),
        in_specs=[pl.BlockSpec((CORES, wide, half), lambda i: (0, 0, 0)), weights, weights, whole],
        out_specs=whole,
        out_shape=jax.ShapeDtypeStruct(got.shape, jnp.bfloat16),
        compiler_params=BIG,
        name="near",
    )(grads_value, keep, sib, got)


def rows_kernel(low_ref, high_ref, keep_ref, sib_ref, *refs):
    def store(grads_ref, more):
        value = chip_sum(grads_ref[...], keep_ref[0], sib_ref[0])
        for ref in more:
            value = value + ref[...].astype(jnp.float32)
        refs[-1][...] = value.astype(refs[-1].dtype)

    @pl.when(pl.program_id(0) == 0)
    def _():
        store(low_ref, (refs[0], refs[2]) if len(refs) > 1 else ())

    @pl.when(pl.program_id(0) == 1)
    def _():
        store(high_ref, (refs[1], refs[2]) if len(refs) > 1 else ())


def all_rows(grads_values, keep, sib, at, more=()):
    _, wide, half = grads_values[0].shape
    _, depth, block = keep.shape
    by_half = pl.BlockSpec((half, block), lambda i: (i, 0))
    whole = pl.BlockSpec((half, block), lambda i: (0, 0))
    weights = pl.BlockSpec((1, depth, block), lambda i: (at, 0, 0))
    return pl.pallas_call(
        rows_kernel,
        grid=(2,),
        in_specs=[pl.BlockSpec((CORES, wide, half), lambda i: (0, 0, 0))] * 2 + [weights, weights] + [whole, whole, by_half][: len(more)],
        out_specs=by_half,
        out_shape=jax.ShapeDtypeStruct((2 * half, block), jnp.bfloat16),
        compiler_params=BIG,
        name="all_rows",
    )(*grads_values, keep, sib, *more)


def combine_kernel(hi_ref, lo_ref, back_ref, out_ref):
    back = back_ref[...]
    value = jnp.dot(hi_ref[...], back, preferred_element_type=jnp.float32)
    value = value + jnp.dot(lo_ref[...], back, preferred_element_type=jnp.float32)
    out_ref[...] = value.astype(out_ref.dtype)


def combine(high, low, back):
    return pl.pallas_call(
        combine_kernel,
        out_shape=jax.ShapeDtypeStruct((high.shape[0], back.shape[1]), jnp.bfloat16),
        name="combine",
    )(high, low, back)


def exchange(rows, n_tok):
    blocks = rows.reshape(n_tok, rows.shape[0] // n_tok, rows.shape[1])
    return lax.all_to_all(blocks, "tok", split_axis=0, concat_axis=0, tiled=True).reshape(rows.shape)


def send(value, to):
    pairs = []
    for i in range(CHIPS * CORES):
        chip, core = to(i // CORES, i % CORES)
        pairs.append((i, chip % CHIPS * CORES + core))
    return lax.ppermute(value, "tp", pairs)


def from_near(value):
    return send(value, lambda chip, core: (chip + 1 - 2 * core, core))


def to_near(value):
    return send(value, lambda chip, core: (chip - 1 + 2 * core, core))


def to_near_other(value):
    return send(value, lambda chip, core: (chip - 1 + 2 * core, 1 - core))


def to_sibling(value):
    return send(value, lambda chip, core: (chip, 1 - core))


def block_order(chip, core):
    near = chip - 1 + 2 * core
    chips = jnp.stack([chip, near, near, chip + 2]) & (CHIPS - 1)
    return chips * CORES + jnp.stack([core, core, 1 - core, core])


def expert(own, weights):
    place = lax.axis_index("tp").astype(jnp.int32)
    chip, core = place >> 1, place & 1
    keep, give = pack(jnp.concatenate([block_order(chip, core), block_order(chip, 1 - core)]), weights)
    sib = to_sibling(give)
    half = own.shape[0] // 2
    halves = (own[:half], own[half:])
    same = [from_near(rows) for rows in halves]
    other = [to_near_other(rows) for rows in halves]
    opposite = [from_near(rows) for rows in same]
    mine = first(own, *same, keep, sib)
    values, far = [], []
    for part in range(2):
        rows = second(other[part], opposite[part], keep, sib, mine, part)
        value, for_opposite = grads(rows, to_sibling(rows), keep, sib)
        values.append(value)
        far.append(to_near(near(value, keep, sib, to_near(for_opposite))))
    from_other = to_near_other(all_rows(values, keep, sib, 2))
    return all_rows(values, keep, sib, 0, (*far, from_other))


def shards(activations, out_grad, routes, gate_vals, w_gate, w_up, w_down):
    n_tok = lax.axis_size("tok")
    tok_dev, top_k = routes.shape
    capacity = max(2, 2 * tok_dev * top_k // n_tok)
    sent = dispatch(routes, activations, out_grad, n_tok, capacity)
    weights, sent, gate_vals = lax.optimization_barrier(((w_gate[0], w_up[0], w_down[0]), sent, gate_vals))
    high, low = mixer(routes, gate_vals, n_tok, capacity)
    own, high, low = lax.optimization_barrier((exchange(sent, n_tok), high, low))
    expert_sum = expert(own, weights)
    return combine(high, low, exchange(expert_sum, n_tok))


def solution(mesh):
    placed = (
        P("tok", "tp"),
        P("tok", "tp"),
        P("tok", None),
        P("tok", None),
        P("tok", "tp", None),
        P("tok", "tp", None),
        P("tok", "tp", None),
    )
    return jax.shard_map(
        shards, mesh=mesh, in_specs=placed, out_specs=P("tok", "tp"), check_vma=False
    )
```

```python
import functools

import jax
import jax.numpy as jnp
from jax import lax
from jax.experimental import pallas as pl
from jax.experimental.pallas import tpu as pltpu
from jax.sharding import PartitionSpec as P

CHIPS = 4
CORES = 2
CONTRACT_LAST = (((1,), (1,)), ((), ()))
BIG = pltpu.CompilerParams(vmem_limit_bytes=40 * 1024 * 1024)


def places(routes_ref, values, n_tok, capacity):
    top_k, tok_dev = routes_ref.shape
    expert = lax.broadcasted_iota(jnp.int32, (n_tok, tok_dev), 0)
    named = jnp.zeros((n_tok, tok_dev), jnp.float32)
    weight = jnp.zeros((n_tok, tok_dev), jnp.float32)
    for k in range(top_k):
        hit = routes_ref[k : k + 1, :] == expert
        named = named + jnp.where(hit, 1.0, 0.0)
        weight = weight + jnp.where(hit, values[k], 0.0)
    earlier = lax.broadcasted_iota(jnp.int32, (tok_dev, tok_dev), 0)
    later = lax.broadcasted_iota(jnp.int32, (tok_dev, tok_dev), 1)
    ahead = jnp.where(earlier < later, 1.0, 0.0).astype(jnp.bfloat16)
    before = jnp.dot(named.astype(jnp.bfloat16), ahead, preferred_element_type=jnp.float32)
    before = jnp.where(named > 0.0, before, -1.0)
    slot = lax.broadcasted_iota(jnp.int32, (n_tok, capacity, tok_dev), 1).astype(jnp.float32)
    placed = jnp.where(before[:, None, :] == slot, weight[:, None, :], 0.0)
    return placed.reshape(n_tok * capacity, tok_dev)


def dispatch_kernel(n_tok, capacity, routes_ref, x_ref, g_ref, send_ref):
    width = x_ref.shape[1]
    placed = places(routes_ref, (1.0,) * routes_ref.shape[0], n_tok, capacity).astype(jnp.bfloat16)
    send_ref[:, :width] = jnp.dot(placed, x_ref[...], preferred_element_type=jnp.float32).astype(send_ref.dtype)
    send_ref[:, width:] = jnp.dot(placed, g_ref[...], preferred_element_type=jnp.float32).astype(send_ref.dtype)


def dispatch(routes, activations, out_grad, n_tok, capacity):
    width = activations.shape[1]
    return pl.pallas_call(
        functools.partial(dispatch_kernel, n_tok, capacity),
        out_shape=jax.ShapeDtypeStruct((n_tok * capacity, 2 * width), activations.dtype),
        name="dispatch",
    )(routes.T, activations, out_grad)


def mixer_kernel(n_tok, capacity, routes_ref, gates_ref, out_ref):
    gates = [gates_ref[k : k + 1, :] for k in range(gates_ref.shape[0])]
    scaled = places(routes_ref, gates, n_tok, capacity).T
    tokens = scaled.shape[0]
    high = scaled.astype(jnp.bfloat16)
    out_ref[:tokens, :] = high
    out_ref[tokens:, :] = (scaled - high.astype(jnp.float32)).astype(jnp.bfloat16)


def mixer(routes, gate_vals, n_tok, capacity):
    return pl.pallas_call(
        functools.partial(mixer_kernel, n_tok, capacity),
        out_shape=jax.ShapeDtypeStruct((2 * routes.shape[0], n_tok * capacity), jnp.bfloat16),
        name="mixer",
    )(routes.T, gate_vals.T)


def pack_kernel(blocks_ref, *refs):
    keep_ref, give_ref = refs[6:]
    hidden = refs[0].shape[0]
    for n in range(3):
        keep_ref[0, n * hidden : (n + 1) * hidden, :] = refs[n][...]
        give_ref[0, n * hidden : (n + 1) * hidden, :] = refs[3 + n][...]


def pack(blocks, weights):
    hidden, width = weights[0].shape
    block = width // (CHIPS * CORES)
    packed = jax.ShapeDtypeStruct((CHIPS, 3 * hidden, block), weights[0].dtype)
    keep = pl.BlockSpec((hidden, block), lambda i, blocks_ref: (0, blocks_ref[i]))
    give = pl.BlockSpec((hidden, block), lambda i, blocks_ref: (0, blocks_ref[i + CHIPS]))
    out = pl.BlockSpec((1, 3 * hidden, block), lambda i, blocks_ref: (i, 0, 0))
    return pl.pallas_call(
        pack_kernel,
        grid_spec=pltpu.PrefetchScalarGridSpec(
            num_scalar_prefetch=1,
            grid=(CHIPS,),
            in_specs=[keep] * 3 + [give] * 3,
            out_specs=[out, out],
        ),
        out_shape=(packed, packed),
        name="pack",
    )(blocks, *weights, *weights)


def products(weight, rows):
    block = weight.shape[1]
    split = weight.shape[0] // 3 * 2
    wide = lax.dot_general(weight[:split], rows[:, :block], CONTRACT_LAST, preferred_element_type=jnp.float32)
    narrow = lax.dot_general(weight[split:], rows[:, block:], CONTRACT_LAST, preferred_element_type=jnp.float32)
    return wide, narrow, split


def first_kernel(own_ref, same_low_ref, same_high_ref, keep_ref, sib_ref, out_ref):
    def store(same_ref):
        for n, weights in enumerate((keep_ref, sib_ref)):
            wide, narrow, split = products(weights[0], own_ref[...])
            same_wide, same_narrow, _ = products(weights[1], same_ref[...])
            out_ref[n, :split, :] = wide + same_wide
            out_ref[n, split:, :] = narrow + same_narrow

    @pl.when(pl.program_id(0) == 0)
    def _():
        store(same_low_ref)

    @pl.when(pl.program_id(0) == 1)
    def _():
        store(same_high_ref)


def first(own, same_low, same_high, keep, sib):
    rows, width = own.shape
    _, depth, block = keep.shape
    half = rows // 2
    whole = pl.BlockSpec((half, width), lambda i: (0, 0))
    weights = pl.BlockSpec((2, depth, block), lambda i: (0, 0, 0))
    return pl.pallas_call(
        first_kernel,
        grid=(2,),
        in_specs=[pl.BlockSpec((half, width), lambda i: (i, 0)), whole, whole, weights, weights],
        out_specs=pl.BlockSpec((CORES, depth, half), lambda i: (0, 0, i)),
        out_shape=jax.ShapeDtypeStruct((CORES, depth, rows), jnp.float32),
        compiler_params=BIG,
        name="first",
    )(own, same_low, same_high, keep, sib)


def second_kernel(other_ref, far_x_ref, far_g_ref, keep_ref, sib_ref, sum_ref, *refs):
    out_ref = refs[-1]
    for n, weights in enumerate((keep_ref, sib_ref)):
        wide, narrow, split = products(weights[0], other_ref[...])
        far = weights[1]
        wide = wide + lax.dot_general(far[:split], far_x_ref[...], CONTRACT_LAST, preferred_element_type=jnp.float32)
        narrow = narrow + lax.dot_general(far[split:], far_g_ref[...], CONTRACT_LAST, preferred_element_type=jnp.float32)
        out_ref[n, :split, :] = sum_ref[n, :split, :] + wide
        out_ref[n, split:, :] = sum_ref[n, split:, :] + narrow


def second(other, opposite, keep, sib, sums, part, before):
    half, width = other.shape
    _, depth, block = keep.shape
    whole = pl.BlockSpec((half, width), lambda i: (0, 0))
    far_x = pl.BlockSpec((half, block), lambda i: (0, 0))
    far_g = pl.BlockSpec((half, block), lambda i: (0, 2 - len(opposite)))
    weights = pl.BlockSpec((2, depth, block), lambda i: (1, 0, 0))
    return pl.pallas_call(
        second_kernel,
        grid=(1,),
        in_specs=[whole, far_x, far_g, weights, weights, pl.BlockSpec((CORES, depth, half), lambda i: (0, 0, part))]
        + [pl.BlockSpec(memory_space=pl.ANY) for _ in before],
        out_specs=pl.BlockSpec((CORES, depth, half), lambda i: (0, 0, 0)),
        out_shape=jax.ShapeDtypeStruct((CORES, depth, half), sums.dtype),
        compiler_params=BIG,
        name="second",
    )(other, opposite[0], opposite[-1], keep, sib, sums, *before)


def chip_sum(grads, keep, sib):
    depth = grads.shape[1]
    return jnp.dot(grads[0].T, keep[:depth, :], preferred_element_type=jnp.float32) + jnp.dot(
        grads[1].T, sib[:depth, :], preferred_element_type=jnp.float32
    )


def grads_kernel(mine_ref, theirs_ref, keep_ref, sib_ref, *refs):
    grads_ref, part_ref = refs[-2:]
    hidden = mine_ref.shape[1] // 3
    for n in range(CORES):
        gate_pre = mine_ref[n, :hidden, :] + theirs_ref[1 - n, :hidden, :]
        up_pre = mine_ref[n, hidden : 2 * hidden, :] + theirs_ref[1 - n, hidden : 2 * hidden, :]
        hidden_grad = mine_ref[n, 2 * hidden :, :] + theirs_ref[1 - n, 2 * hidden :, :]
        sigma = 1.0 / (1.0 + jnp.exp(-gate_pre))
        slope = sigma * (1.0 + gate_pre * (1.0 - sigma))
        grads_ref[n, :hidden, :] = (hidden_grad * up_pre * slope).astype(grads_ref.dtype)
        grads_ref[n, hidden:, :] = (hidden_grad * (gate_pre * sigma)).astype(grads_ref.dtype)
    part_ref[...] = chip_sum(grads_ref[...], keep_ref[0], sib_ref[0]).astype(part_ref.dtype)


def grads(mine, theirs, keep, sib, before):
    _, depth, half = mine.shape
    block = keep.shape[2]
    wide = depth // 3 * 2
    whole = pl.BlockSpec((CORES, depth, half), lambda i: (0, 0, 0))
    weights = pl.BlockSpec((1, depth, block), lambda i: (CHIPS - 1, 0, 0))
    return pl.pallas_call(
        grads_kernel,
        grid=(1,),
        in_specs=[whole, whole, weights, weights] + [pl.BlockSpec(memory_space=pl.ANY) for _ in before],
        out_specs=[pl.BlockSpec((CORES, wide, half), lambda i: (0, 0, 0)), pl.BlockSpec((half, block), lambda i: (0, 0))],
        out_shape=(jax.ShapeDtypeStruct((CORES, wide, half), jnp.bfloat16), jax.ShapeDtypeStruct((half, block), jnp.bfloat16)),
        compiler_params=BIG,
        name="grads",
    )(mine, theirs, keep, sib, *before)


def near_kernel(grads_ref, keep_ref, sib_ref, got_ref, *refs):
    out_ref = refs[-1]
    value = chip_sum(grads_ref[...], keep_ref[0], sib_ref[0]) + got_ref[...].astype(jnp.float32)
    out_ref[...] = value.astype(out_ref.dtype)


def near(grads_value, keep, sib, got, before):
    _, wide, half = grads_value.shape
    _, depth, block = keep.shape
    weights = pl.BlockSpec((1, depth, block), lambda i: (1, 0, 0))
    whole = pl.BlockSpec((half, block), lambda i: (0, 0))
    return pl.pallas_call(
        near_kernel,
        grid=(1,),
        in_specs=[pl.BlockSpec((CORES, wide, half), lambda i: (0, 0, 0)), weights, weights, whole]
        + [pl.BlockSpec(memory_space=pl.ANY) for _ in before],
        out_specs=whole,
        out_shape=jax.ShapeDtypeStruct(got.shape, jnp.bfloat16),
        compiler_params=BIG,
        name="near",
    )(grads_value, keep, sib, got, *before)


def other_kernel(low_ref, high_ref, keep_ref, sib_ref, out_ref):
    @pl.when(pl.program_id(0) == 0)
    def _():
        out_ref[...] = chip_sum(low_ref[...], keep_ref[0], sib_ref[0]).astype(out_ref.dtype)

    @pl.when(pl.program_id(0) == 1)
    def _():
        out_ref[...] = chip_sum(high_ref[...], keep_ref[0], sib_ref[0]).astype(out_ref.dtype)


def for_other(grads_values, keep, sib):
    _, wide, half = grads_values[0].shape
    _, depth, block = keep.shape
    weights = pl.BlockSpec((1, depth, block), lambda i: (2, 0, 0))
    return pl.pallas_call(
        other_kernel,
        grid=(2,),
        in_specs=[pl.BlockSpec((CORES, wide, half), lambda i: (0, 0, 0))] * 2 + [weights, weights],
        out_specs=pl.BlockSpec((half, block), lambda i: (i, 0)),
        out_shape=jax.ShapeDtypeStruct((2 * half, block), jnp.bfloat16),
        compiler_params=BIG,
        name="for_other",
    )(*grads_values, keep, sib)


def total_kernel(grads_ref, keep_ref, sib_ref, far_ref, other_ref, *refs):
    value = chip_sum(grads_ref[...], keep_ref[0], sib_ref[0])
    value = value + far_ref[...].astype(jnp.float32) + other_ref[...].astype(jnp.float32)
    refs[-1][...] = value.astype(refs[-1].dtype)


def total(grads_value, keep, sib, far, other, part, before):
    _, wide, half = grads_value.shape
    _, depth, block = keep.shape
    weights = pl.BlockSpec((1, depth, block), lambda i: (0, 0, 0))
    by_part = pl.BlockSpec((half, block), lambda i: (part, 0))
    return pl.pallas_call(
        total_kernel,
        grid=(1,),
        in_specs=[
            pl.BlockSpec((CORES, wide, half), lambda i: (0, 0, 0)),
            weights,
            weights,
            pl.BlockSpec((half, block), lambda i: (0, 0)),
            by_part,
        ]
        + [pl.BlockSpec(memory_space=pl.ANY) for _ in before],
        out_specs=by_part,
        out_shape=jax.ShapeDtypeStruct(other.shape, jnp.bfloat16),
        input_output_aliases={5: 0} if before else {},
        compiler_params=BIG,
        name="total",
    )(grads_value, keep, sib, far, other, *before)


def combine_kernel(mix_ref, back_ref, out_ref):
    tokens = out_ref.shape[0]
    value = jnp.dot(mix_ref[...], back_ref[...], preferred_element_type=jnp.float32)
    out_ref[...] = (value[:tokens] + value[tokens:]).astype(out_ref.dtype)


def combine(mix, back):
    return pl.pallas_call(
        combine_kernel,
        out_shape=jax.ShapeDtypeStruct((mix.shape[0] // 2, back.shape[1]), jnp.bfloat16),
        name="combine",
    )(mix, back)


def exchange(rows, n_tok):
    blocks = rows.reshape(n_tok, rows.shape[0] // n_tok, rows.shape[1])
    return lax.all_to_all(blocks, "tok", split_axis=0, concat_axis=0, tiled=True).reshape(rows.shape)


def send(value, to):
    pairs = []
    for i in range(CHIPS * CORES):
        chip, core = to(i // CORES, i % CORES)
        pairs.append((i, chip % CHIPS * CORES + core))
    return lax.ppermute(value, "tp", pairs)


def from_near(value):
    return send(value, lambda chip, core: (chip + 1 - 2 * core, core))


def to_near(value):
    return send(value, lambda chip, core: (chip - 1 + 2 * core, core))


def to_near_other(value):
    return send(value, lambda chip, core: (chip - 1 + 2 * core, 1 - core))


def to_sibling(value):
    return send(value, lambda chip, core: (chip, 1 - core))


def block_order(chip, core):
    near = chip - 1 + 2 * core
    chips = jnp.stack([chip, near, near, chip + 2]) & (CHIPS - 1)
    return chips * CORES + jnp.stack([core, core, 1 - core, core])


def expert(own, weights):
    place = lax.axis_index("tp").astype(jnp.int32)
    chip, core = place >> 1, place & 1
    keep, give = pack(jnp.concatenate([block_order(chip, core), block_order(chip, 1 - core)]), weights)
    sib = to_sibling(give)
    half = own.shape[0] // 2
    halves = (own[:half], own[half:])
    same = [from_near(rows) for rows in halves]
    other = [to_near_other(rows) for rows in halves]
    width = own.shape[1] // 2
    opposite = [(from_near(same[0]),), (from_near(same[1][:, :width]), from_near(same[1][:, width:]))]
    mine = first(own, *same, keep, sib)
    values, passed, far, earlier = [], [], [], []
    for part in range(2):
        rows = second(other[part], opposite[part], keep, sib, mine, part, earlier)
        earlier = [rows]
        value, for_opposite = grads(rows, to_sibling(rows), keep, sib, values)
        values.append(value)
        passed.append(near(value, keep, sib, to_near(for_opposite), tuple(passed)))
        far.append(to_near(passed[-1]))
    from_other = to_near_other(for_other(values, keep, sib))
    low = total(values[0], keep, sib, far[0], from_other, 0, ())
    return total(values[1], keep, sib, far[1], from_other, 1, (low,))


def shards(activations, out_grad, routes, gate_vals, w_gate, w_up, w_down):
    n_tok = lax.axis_size("tok")
    tok_dev, top_k = routes.shape
    capacity = max(2, 2 * tok_dev * top_k // n_tok)
    sent = dispatch(routes, activations, out_grad, n_tok, capacity)
    weights, sent, gate_vals = lax.optimization_barrier(((w_gate[0], w_up[0], w_down[0]), sent, gate_vals))
    mix = mixer(routes, gate_vals, n_tok, capacity)
    own, mix = lax.optimization_barrier((exchange(sent, n_tok), mix))
    expert_sum = expert(own, weights)
    return combine(mix, exchange(expert_sum, n_tok))


def solution(mesh):
    placed = (
        P("tok", "tp"),
        P("tok", "tp"),
        P("tok", None),
        P("tok", None),
        P("tok", "tp", None),
        P("tok", "tp", None),
        P("tok", "tp", None),
    )
    return jax.shard_map(
        shards, mesh=mesh, in_specs=placed, out_specs=P("tok", "tp"), check_vma=False
    )
```

```python
import functools

import jax
import jax.numpy as jnp
from jax import lax
from jax.experimental import pallas as pl
from jax.experimental.pallas import tpu as pltpu
from jax.sharding import PartitionSpec as P

CHIPS = 4
CORES = 2
CONTRACT_LAST = (((1,), (1,)), ((), ()))
BIG = pltpu.CompilerParams(vmem_limit_bytes=40 * 1024 * 1024)


def places(routes_ref, values, n_tok, capacity):
    top_k, tok_dev = routes_ref.shape
    expert = lax.broadcasted_iota(jnp.int32, (n_tok, tok_dev), 0)
    named = jnp.zeros((n_tok, tok_dev), jnp.float32)
    weight = jnp.zeros((n_tok, tok_dev), jnp.float32)
    for k in range(top_k):
        hit = routes_ref[k : k + 1, :] == expert
        named = named + jnp.where(hit, 1.0, 0.0)
        weight = weight + jnp.where(hit, values[k], 0.0)
    earlier = lax.broadcasted_iota(jnp.int32, (tok_dev, tok_dev), 0)
    later = lax.broadcasted_iota(jnp.int32, (tok_dev, tok_dev), 1)
    ahead = jnp.where(earlier < later, 1.0, 0.0).astype(jnp.bfloat16)
    before = jnp.dot(named.astype(jnp.bfloat16), ahead, preferred_element_type=jnp.float32)
    before = jnp.where(named > 0.0, before, -1.0)
    slot = lax.broadcasted_iota(jnp.int32, (n_tok, capacity, tok_dev), 1).astype(jnp.float32)
    placed = jnp.where(before[:, None, :] == slot, weight[:, None, :], 0.0)
    return placed.reshape(n_tok * capacity, tok_dev)


def dispatch_kernel(n_tok, capacity, routes_ref, x_ref, g_ref, send_ref):
    width = x_ref.shape[1]
    placed = places(routes_ref, (1.0,) * routes_ref.shape[0], n_tok, capacity).astype(jnp.bfloat16)
    send_ref[:, :width] = jnp.dot(placed, x_ref[...], preferred_element_type=jnp.float32).astype(send_ref.dtype)
    send_ref[:, width:] = jnp.dot(placed, g_ref[...], preferred_element_type=jnp.float32).astype(send_ref.dtype)


def dispatch(routes, activations, out_grad, n_tok, capacity):
    width = activations.shape[1]
    return pl.pallas_call(
        functools.partial(dispatch_kernel, n_tok, capacity),
        out_shape=jax.ShapeDtypeStruct((n_tok * capacity, 2 * width), activations.dtype),
        name="dispatch",
    )(routes.T, activations, out_grad)


def mixer_kernel(n_tok, capacity, routes_ref, gates_ref, hi_ref, lo_ref):
    gates = [gates_ref[k : k + 1, :] for k in range(gates_ref.shape[0])]
    scaled = places(routes_ref, gates, n_tok, capacity).T
    high = scaled.astype(jnp.bfloat16)
    hi_ref[...] = high
    lo_ref[...] = (scaled - high.astype(jnp.float32)).astype(jnp.bfloat16)


def mixer(routes, gate_vals, n_tok, capacity):
    part = jax.ShapeDtypeStruct((routes.shape[0], n_tok * capacity), jnp.bfloat16)
    return pl.pallas_call(
        functools.partial(mixer_kernel, n_tok, capacity),
        out_shape=(part, part),
        name="mixer",
    )(routes.T, gate_vals.T)


def pack_kernel(blocks_ref, *refs):
    keep_ref, give_ref = refs[6:]
    hidden = refs[0].shape[0]
    for n in range(3):
        keep_ref[0, n * hidden : (n + 1) * hidden, :] = refs[n][...]
        give_ref[0, n * hidden : (n + 1) * hidden, :] = refs[3 + n][...]


def pack(blocks, weights):
    hidden, width = weights[0].shape
    block = width // (CHIPS * CORES)
    packed = jax.ShapeDtypeStruct((CHIPS, 3 * hidden, block), weights[0].dtype)
    keep = pl.BlockSpec((hidden, block), lambda i, blocks_ref: (0, blocks_ref[i]))
    give = pl.BlockSpec((hidden, block), lambda i, blocks_ref: (0, blocks_ref[i + CHIPS]))
    out = pl.BlockSpec((1, 3 * hidden, block), lambda i, blocks_ref: (i, 0, 0))
    return pl.pallas_call(
        pack_kernel,
        grid_spec=pltpu.PrefetchScalarGridSpec(
            num_scalar_prefetch=1,
            grid=(CHIPS,),
            in_specs=[keep] * 3 + [give] * 3,
            out_specs=[out, out],
        ),
        out_shape=(packed, packed),
        name="pack",
    )(blocks, *weights, *weights)


def products(weight, rows):
    block = weight.shape[1]
    split = weight.shape[0] // 3 * 2
    wide = lax.dot_general(weight[:split], rows[:, :block], CONTRACT_LAST, preferred_element_type=jnp.float32)
    narrow = lax.dot_general(weight[split:], rows[:, block:], CONTRACT_LAST, preferred_element_type=jnp.float32)
    return wide, narrow, split


def first_kernel(own_ref, same_low_ref, same_high_ref, keep_ref, sib_ref, out_ref):
    def store(same_ref):
        for n, weights in enumerate((keep_ref, sib_ref)):
            wide, narrow, split = products(weights[0], own_ref[...])
            same_wide, same_narrow, _ = products(weights[1], same_ref[...])
            out_ref[n, :split, :] = wide + same_wide
            out_ref[n, split:, :] = narrow + same_narrow

    @pl.when(pl.program_id(0) == 0)
    def _():
        store(same_low_ref)

    @pl.when(pl.program_id(0) == 1)
    def _():
        store(same_high_ref)


def first(own, same_low, same_high, keep, sib):
    rows, width = own.shape
    _, depth, block = keep.shape
    half = rows // 2
    whole = pl.BlockSpec((half, width), lambda i: (0, 0))
    weights = pl.BlockSpec((2, depth, block), lambda i: (0, 0, 0))
    return pl.pallas_call(
        first_kernel,
        grid=(2,),
        in_specs=[pl.BlockSpec((half, width), lambda i: (i, 0)), whole, whole, weights, weights],
        out_specs=pl.BlockSpec((CORES, depth, half), lambda i: (0, 0, i)),
        out_shape=jax.ShapeDtypeStruct((CORES, depth, rows), jnp.float32),
        compiler_params=BIG,
        name="first",
    )(own, same_low, same_high, keep, sib)


def second_kernel(other_ref, opposite_ref, keep_ref, sib_ref, sum_ref, out_ref):
    for n, weights in enumerate((keep_ref, sib_ref)):
        wide, narrow, split = products(weights[0], other_ref[...])
        far_wide, far_narrow, _ = products(weights[1], opposite_ref[...])
        out_ref[n, :split, :] = sum_ref[n, :split, :] + (wide + far_wide)
        out_ref[n, split:, :] = sum_ref[n, split:, :] + (narrow + far_narrow)


def second(other, opposite, keep, sib, sums, part):
    half, width = other.shape
    _, depth, block = keep.shape
    whole = pl.BlockSpec((half, width), lambda i: (0, 0))
    weights = pl.BlockSpec((2, depth, block), lambda i: (1, 0, 0))
    return pl.pallas_call(
        second_kernel,
        grid=(1,),
        in_specs=[whole, whole, weights, weights, pl.BlockSpec((CORES, depth, half), lambda i: (0, 0, part))],
        out_specs=pl.BlockSpec((CORES, depth, half), lambda i: (0, 0, 0)),
        out_shape=jax.ShapeDtypeStruct((CORES, depth, half), sums.dtype),
        compiler_params=BIG,
        name="second",
    )(other, opposite, keep, sib, sums)


def chip_sum(grads, keep, sib):
    depth = grads.shape[1]
    return jnp.dot(grads[0].T, keep[:depth, :], preferred_element_type=jnp.float32) + jnp.dot(
        grads[1].T, sib[:depth, :], preferred_element_type=jnp.float32
    )


def grads_kernel(mine_ref, theirs_ref, keep_ref, sib_ref, grads_ref, part_ref, other_ref):
    hidden = mine_ref.shape[1] // 3
    for n in range(CORES):
        gate_pre = mine_ref[n, :hidden, :] + theirs_ref[1 - n, :hidden, :]
        up_pre = mine_ref[n, hidden : 2 * hidden, :] + theirs_ref[1 - n, hidden : 2 * hidden, :]
        hidden_grad = mine_ref[n, 2 * hidden :, :] + theirs_ref[1 - n, 2 * hidden :, :]
        sigma = 1.0 / (1.0 + jnp.exp(-gate_pre))
        slope = sigma * (1.0 + gate_pre * (1.0 - sigma))
        grads_ref[n, :hidden, :] = (hidden_grad * up_pre * slope).astype(grads_ref.dtype)
        grads_ref[n, hidden:, :] = (hidden_grad * (gate_pre * sigma)).astype(grads_ref.dtype)
    part_ref[...] = chip_sum(grads_ref[...], keep_ref[1], sib_ref[1]).astype(part_ref.dtype)
    other_ref[...] = chip_sum(grads_ref[...], keep_ref[0], sib_ref[0]).astype(other_ref.dtype)


def grads(mine, theirs, keep, sib):
    _, depth, half = mine.shape
    block = keep.shape[2]
    wide = depth // 3 * 2
    whole = pl.BlockSpec((CORES, depth, half), lambda i: (0, 0, 0))
    weights = pl.BlockSpec((2, depth, block), lambda i: (1, 0, 0))
    out = pl.BlockSpec((half, block), lambda i: (0, 0))
    part = jax.ShapeDtypeStruct((half, block), jnp.bfloat16)
    return pl.pallas_call(
        grads_kernel,
        grid=(1,),
        in_specs=[whole, whole, weights, weights],
        out_specs=[pl.BlockSpec((CORES, wide, half), lambda i: (0, 0, 0)), out, out],
        out_shape=(jax.ShapeDtypeStruct((CORES, wide, half), jnp.bfloat16), part, part),
        compiler_params=BIG,
        name="grads",
    )(mine, theirs, keep, sib)


def near_kernel(grads_ref, keep_ref, sib_ref, got_ref, out_ref):
    value = chip_sum(grads_ref[...], keep_ref[0], sib_ref[0]) + got_ref[...].astype(jnp.float32)
    out_ref[...] = value.astype(out_ref.dtype)


def near(grads_value, keep, sib, got):
    _, wide, half = grads_value.shape
    _, depth, block = keep.shape
    weights = pl.BlockSpec((1, depth, block), lambda i: (1, 0, 0))
    whole = pl.BlockSpec((half, block), lambda i: (0, 0))
    return pl.pallas_call(
        near_kernel,
        grid=(1,),
        in_specs=[pl.BlockSpec((CORES, wide, half), lambda i: (0, 0, 0)), weights, weights, whole],
        out_specs=whole,
        out_shape=jax.ShapeDtypeStruct(got.shape, jnp.bfloat16),
        compiler_params=BIG,
        name="near",
    )(grads_value, keep, sib, got)


def total_kernel(low_ref, high_ref, keep_ref, sib_ref, *refs):
    def store(grads_ref, far_ref, other_ref):
        value = chip_sum(grads_ref[...], keep_ref[0], sib_ref[0])
        value = value + far_ref[...].astype(jnp.float32) + other_ref[...].astype(jnp.float32)
        refs[-1][...] = value.astype(refs[-1].dtype)

    @pl.when(pl.program_id(0) == 0)
    def _():
        store(low_ref, refs[0], refs[1])

    @pl.when(pl.program_id(0) == 1)
    def _():
        store(high_ref, refs[2], refs[3])


def total(grads_values, keep, sib, more):
    _, wide, half = grads_values[0].shape
    _, depth, block = keep.shape
    whole = pl.BlockSpec((half, block), lambda i: (0, 0))
    weights = pl.BlockSpec((1, depth, block), lambda i: (0, 0, 0))
    return pl.pallas_call(
        total_kernel,
        grid=(2,),
        in_specs=[pl.BlockSpec((CORES, wide, half), lambda i: (0, 0, 0))] * 2 + [weights, weights] + [whole] * 4,
        out_specs=pl.BlockSpec((half, block), lambda i: (i, 0)),
        out_shape=jax.ShapeDtypeStruct((2 * half, block), jnp.bfloat16),
        compiler_params=BIG,
        name="total",
    )(*grads_values, keep, sib, *more)


def combine_kernel(hi_ref, lo_ref, back_ref, out_ref):
    back = back_ref[...]
    value = jnp.dot(hi_ref[...], back, preferred_element_type=jnp.float32)
    value = value + jnp.dot(lo_ref[...], back, preferred_element_type=jnp.float32)
    out_ref[...] = value.astype(out_ref.dtype)


def combine(high, low, back):
    return pl.pallas_call(
        combine_kernel,
        out_shape=jax.ShapeDtypeStruct((high.shape[0], back.shape[1]), jnp.bfloat16),
        name="combine",
    )(high, low, back)


def exchange(rows, n_tok):
    blocks = rows.reshape(n_tok, rows.shape[0] // n_tok, rows.shape[1])
    return lax.all_to_all(blocks, "tok", split_axis=0, concat_axis=0, tiled=True).reshape(rows.shape)


def send(value, to):
    pairs = []
    for i in range(CHIPS * CORES):
        chip, core = to(i // CORES, i % CORES)
        pairs.append((i, chip % CHIPS * CORES + core))
    return lax.ppermute(value, "tp", pairs)


def from_near(value):
    return send(value, lambda chip, core: (chip + 1 - 2 * core, core))


def to_near(value):
    return send(value, lambda chip, core: (chip - 1 + 2 * core, core))


def to_near_other(value):
    return send(value, lambda chip, core: (chip - 1 + 2 * core, 1 - core))


def to_sibling(value):
    return send(value, lambda chip, core: (chip, 1 - core))


def block_order(chip, core):
    near = chip - 1 + 2 * core
    chips = jnp.stack([chip, near, near, chip + 2]) & (CHIPS - 1)
    return chips * CORES + jnp.stack([core, core, 1 - core, core])


def expert(own, weights):
    place = lax.axis_index("tp").astype(jnp.int32)
    chip, core = place >> 1, place & 1
    keep, give = pack(jnp.concatenate([block_order(chip, core), block_order(chip, 1 - core)]), weights)
    sib = to_sibling(give)
    half = own.shape[0] // 2
    halves = (own[:half], own[half:])
    same = [from_near(rows) for rows in halves]
    other = [to_near_other(rows) for rows in halves]
    opposite = [from_near(rows) for rows in same]
    mine = first(own, *same, keep, sib)
    values, more = [], []
    for part in range(2):
        rows = second(other[part], opposite[part], keep, sib, mine, part)
        value, for_opposite, for_other = grads(rows, to_sibling(rows), keep, sib)
        values.append(value)
        more += [to_near(near(value, keep, sib, to_near(for_opposite))), to_near_other(for_other)]
    return total(values, keep, sib, more)


def shards(activations, out_grad, routes, gate_vals, w_gate, w_up, w_down):
    n_tok = lax.axis_size("tok")
    tok_dev, top_k = routes.shape
    capacity = max(2, 2 * tok_dev * top_k // n_tok)
    sent = dispatch(routes, activations, out_grad, n_tok, capacity)
    weights, sent, gate_vals = lax.optimization_barrier(((w_gate[0], w_up[0], w_down[0]), sent, gate_vals))
    high, low = mixer(routes, gate_vals, n_tok, capacity)
    own, high, low = lax.optimization_barrier((exchange(sent, n_tok), high, low))
    expert_sum = expert(own, weights)
    return combine(high, low, exchange(expert_sum, n_tok))


def solution(mesh):
    placed = (
        P("tok", "tp"),
        P("tok", "tp"),
        P("tok", None),
        P("tok", None),
        P("tok", "tp", None),
        P("tok", "tp", None),
        P("tok", "tp", None),
    )
    return jax.shard_map(
        shards, mesh=mesh, in_specs=placed, out_specs=P("tok", "tp"), check_vma=False
    )
```

```python
import functools

import jax
import jax.numpy as jnp
from jax import lax
from jax.experimental import pallas as pl
from jax.experimental.pallas import tpu as pltpu
from jax.sharding import PartitionSpec as P

CHIPS = 4
CORES = 2
CONTRACT_LAST = (((1,), (1,)), ((), ()))
BIG = pltpu.CompilerParams(vmem_limit_bytes=40 * 1024 * 1024)


def places(routes_ref, values, n_tok, capacity):
    top_k, tok_dev = routes_ref.shape
    expert = lax.broadcasted_iota(jnp.int32, (n_tok, tok_dev), 0)
    named = jnp.zeros((n_tok, tok_dev), jnp.float32)
    weight = jnp.zeros((n_tok, tok_dev), jnp.float32)
    for k in range(top_k):
        hit = routes_ref[k : k + 1, :] == expert
        named = named + jnp.where(hit, 1.0, 0.0)
        weight = weight + jnp.where(hit, values[k], 0.0)
    earlier = lax.broadcasted_iota(jnp.int32, (tok_dev, tok_dev), 0)
    later = lax.broadcasted_iota(jnp.int32, (tok_dev, tok_dev), 1)
    ahead = jnp.where(earlier < later, 1.0, 0.0).astype(jnp.bfloat16)
    before = jnp.dot(named.astype(jnp.bfloat16), ahead, preferred_element_type=jnp.float32)
    before = jnp.where(named > 0.0, before, -1.0)
    slot = lax.broadcasted_iota(jnp.int32, (n_tok, capacity, tok_dev), 1).astype(jnp.float32)
    placed = jnp.where(before[:, None, :] == slot, weight[:, None, :], 0.0)
    return placed.reshape(n_tok * capacity, tok_dev)


def dispatch_kernel(n_tok, capacity, routes_ref, x_ref, g_ref, send_ref):
    width = x_ref.shape[1]
    placed = places(routes_ref, (1.0,) * routes_ref.shape[0], n_tok, capacity).astype(jnp.bfloat16)
    send_ref[:, :width] = jnp.dot(placed, x_ref[...], preferred_element_type=jnp.float32).astype(send_ref.dtype)
    send_ref[:, width:] = jnp.dot(placed, g_ref[...], preferred_element_type=jnp.float32).astype(send_ref.dtype)


def dispatch(routes, activations, out_grad, n_tok, capacity):
    width = activations.shape[1]
    return pl.pallas_call(
        functools.partial(dispatch_kernel, n_tok, capacity),
        out_shape=jax.ShapeDtypeStruct((n_tok * capacity, 2 * width), activations.dtype),
        name="dispatch",
    )(routes.T, activations, out_grad)


def mixer_kernel(n_tok, capacity, routes_ref, gates_ref, hi_ref, lo_ref):
    gates = [gates_ref[k : k + 1, :] for k in range(gates_ref.shape[0])]
    scaled = places(routes_ref, gates, n_tok, capacity).T
    high = scaled.astype(jnp.bfloat16)
    hi_ref[...] = high
    lo_ref[...] = (scaled - high.astype(jnp.float32)).astype(jnp.bfloat16)


def mixer(routes, gate_vals, n_tok, capacity):
    part = jax.ShapeDtypeStruct((routes.shape[0], n_tok * capacity), jnp.bfloat16)
    return pl.pallas_call(
        functools.partial(mixer_kernel, n_tok, capacity),
        out_shape=(part, part),
        name="mixer",
    )(routes.T, gate_vals.T)


def pack_kernel(blocks_ref, *refs):
    keep_ref, give_ref = refs[6:]
    hidden = refs[0].shape[0]
    for n in range(3):
        keep_ref[0, n * hidden : (n + 1) * hidden, :] = refs[n][...]
        give_ref[0, n * hidden : (n + 1) * hidden, :] = refs[3 + n][...]


def pack(blocks, weights):
    hidden, width = weights[0].shape
    block = width // (CHIPS * CORES)
    packed = jax.ShapeDtypeStruct((CHIPS, 3 * hidden, block), weights[0].dtype)
    keep = pl.BlockSpec((hidden, block), lambda i, blocks_ref: (0, blocks_ref[i]))
    give = pl.BlockSpec((hidden, block), lambda i, blocks_ref: (0, blocks_ref[i + CHIPS]))
    out = pl.BlockSpec((1, 3 * hidden, block), lambda i, blocks_ref: (i, 0, 0))
    return pl.pallas_call(
        pack_kernel,
        grid_spec=pltpu.PrefetchScalarGridSpec(
            num_scalar_prefetch=1,
            grid=(CHIPS,),
            in_specs=[keep] * 3 + [give] * 3,
            out_specs=[out, out],
        ),
        out_shape=(packed, packed),
        name="pack",
    )(blocks, *weights, *weights)


def products(weight, rows):
    block = weight.shape[1]
    split = weight.shape[0] // 3 * 2
    wide = lax.dot_general(weight[:split], rows[:, :block], CONTRACT_LAST, preferred_element_type=jnp.float32)
    narrow = lax.dot_general(weight[split:], rows[:, block:], CONTRACT_LAST, preferred_element_type=jnp.float32)
    return wide, narrow, split


def first_kernel(own_ref, same_low_ref, same_high_ref, keep_ref, sib_ref, out_ref):
    def store(same_ref):
        for n, weights in enumerate((keep_ref, sib_ref)):
            wide, narrow, split = products(weights[0], own_ref[...])
            same_wide, same_narrow, _ = products(weights[1], same_ref[...])
            out_ref[n, :split, :] = wide + same_wide
            out_ref[n, split:, :] = narrow + same_narrow

    @pl.when(pl.program_id(0) == 0)
    def _():
        store(same_low_ref)

    @pl.when(pl.program_id(0) == 1)
    def _():
        store(same_high_ref)


def first(own, same_low, same_high, keep, sib):
    rows, width = own.shape
    _, depth, block = keep.shape
    half = rows // 2
    whole = pl.BlockSpec((half, width), lambda i: (0, 0))
    weights = pl.BlockSpec((2, depth, block), lambda i: (0, 0, 0))
    return pl.pallas_call(
        first_kernel,
        grid=(2,),
        in_specs=[pl.BlockSpec((half, width), lambda i: (i, 0)), whole, whole, weights, weights],
        out_specs=pl.BlockSpec((CORES, depth, half), lambda i: (0, 0, i)),
        out_shape=jax.ShapeDtypeStruct((CORES, depth, rows), jnp.float32),
        compiler_params=BIG,
        name="first",
    )(own, same_low, same_high, keep, sib)


def second_kernel(other_ref, opposite_ref, keep_ref, sib_ref, sum_ref, out_ref):
    for n, weights in enumerate((keep_ref, sib_ref)):
        wide, narrow, split = products(weights[0], other_ref[...])
        far_wide, far_narrow, _ = products(weights[1], opposite_ref[...])
        out_ref[n, :split, :] = sum_ref[n, :split, :] + (wide + far_wide)
        out_ref[n, split:, :] = sum_ref[n, split:, :] + (narrow + far_narrow)


def second(other, opposite, keep, sib, sums, part):
    half, width = other.shape
    _, depth, block = keep.shape
    whole = pl.BlockSpec((half, width), lambda i: (0, 0))
    weights = pl.BlockSpec((2, depth, block), lambda i: (1, 0, 0))
    return pl.pallas_call(
        second_kernel,
        grid=(1,),
        in_specs=[whole, whole, weights, weights, pl.BlockSpec((CORES, depth, half), lambda i: (0, 0, part))],
        out_specs=pl.BlockSpec((CORES, depth, half), lambda i: (0, 0, 0)),
        out_shape=jax.ShapeDtypeStruct((CORES, depth, half), sums.dtype),
        compiler_params=BIG,
        name="second",
    )(other, opposite, keep, sib, sums)


def chip_sum(grads, keep, sib):
    depth = grads.shape[1]
    return jnp.dot(grads[0].T, keep[:depth, :], preferred_element_type=jnp.float32) + jnp.dot(
        grads[1].T, sib[:depth, :], preferred_element_type=jnp.float32
    )


def grads_kernel(mine_ref, theirs_ref, keep_ref, sib_ref, *refs):
    grads_ref, part_ref, other_ref = refs[-3:]
    hidden = mine_ref.shape[1] // 3
    for n in range(CORES):
        gate_pre = mine_ref[n, :hidden, :] + theirs_ref[1 - n, :hidden, :]
        up_pre = mine_ref[n, hidden : 2 * hidden, :] + theirs_ref[1 - n, hidden : 2 * hidden, :]
        hidden_grad = mine_ref[n, 2 * hidden :, :] + theirs_ref[1 - n, 2 * hidden :, :]
        sigma = 1.0 / (1.0 + jnp.exp(-gate_pre))
        slope = sigma * (1.0 + gate_pre * (1.0 - sigma))
        grads_ref[n, :hidden, :] = (hidden_grad * up_pre * slope).astype(grads_ref.dtype)
        grads_ref[n, hidden:, :] = (hidden_grad * (gate_pre * sigma)).astype(grads_ref.dtype)
    part_ref[...] = chip_sum(grads_ref[...], keep_ref[1], sib_ref[1]).astype(part_ref.dtype)
    other_ref[...] = chip_sum(grads_ref[...], keep_ref[0], sib_ref[0]).astype(other_ref.dtype)


def grads(mine, theirs, keep, sib, at, before):
    _, depth, half = mine.shape
    block = keep.shape[2]
    wide = depth // 3 * 2
    whole = pl.BlockSpec((CORES, depth, half), lambda i: (0, 0, 0))
    weights = pl.BlockSpec((2, depth, block), lambda i: (1, 0, 0))
    out = pl.BlockSpec((half, block), lambda i: (0, 0))
    part = jax.ShapeDtypeStruct((half, block), jnp.bfloat16)
    return pl.pallas_call(
        grads_kernel,
        grid=(1,),
        in_specs=[whole, whole, weights, weights] + [pl.BlockSpec(memory_space=pl.ANY) for _ in before],
        out_specs=[pl.BlockSpec((CORES, wide, half), lambda i: (0, 0, 0)), out, pl.BlockSpec((half, block), lambda i: (at, 0))],
        out_shape=(jax.ShapeDtypeStruct((CORES, wide, half), jnp.bfloat16), part, jax.ShapeDtypeStruct((2 * half, block), jnp.bfloat16)),
        input_output_aliases={4: 2} if before else {},
        compiler_params=BIG,
        name="grads",
    )(mine, theirs, keep, sib, *before)


def near_kernel(grads_ref, keep_ref, sib_ref, got_ref, out_ref):
    value = chip_sum(grads_ref[...], keep_ref[0], sib_ref[0]) + got_ref[...].astype(jnp.float32)
    out_ref[...] = value.astype(out_ref.dtype)


def near(grads_value, keep, sib, got):
    _, wide, half = grads_value.shape
    _, depth, block = keep.shape
    weights = pl.BlockSpec((1, depth, block), lambda i: (1, 0, 0))
    whole = pl.BlockSpec((half, block), lambda i: (0, 0))
    return pl.pallas_call(
        near_kernel,
        grid=(1,),
        in_specs=[pl.BlockSpec((CORES, wide, half), lambda i: (0, 0, 0)), weights, weights, whole],
        out_specs=whole,
        out_shape=jax.ShapeDtypeStruct(got.shape, jnp.bfloat16),
        compiler_params=BIG,
        name="near",
    )(grads_value, keep, sib, got)


def total_kernel(low_ref, high_ref, keep_ref, sib_ref, *refs):
    def store(grads_ref, far_ref, other_ref):
        value = chip_sum(grads_ref[...], keep_ref[0], sib_ref[0])
        value = value + far_ref[...].astype(jnp.float32) + other_ref[...].astype(jnp.float32)
        refs[-1][...] = value.astype(refs[-1].dtype)

    @pl.when(pl.program_id(0) == 0)
    def _():
        store(low_ref, refs[0], refs[2])

    @pl.when(pl.program_id(0) == 1)
    def _():
        store(high_ref, refs[1], refs[2])


def total(grads_values, keep, sib, more):
    _, wide, half = grads_values[0].shape
    _, depth, block = keep.shape
    whole = pl.BlockSpec((half, block), lambda i: (0, 0))
    weights = pl.BlockSpec((1, depth, block), lambda i: (0, 0, 0))
    return pl.pallas_call(
        total_kernel,
        grid=(2,),
        in_specs=[pl.BlockSpec((CORES, wide, half), lambda i: (0, 0, 0))] * 2 + [weights, weights] + [whole, whole, pl.BlockSpec((half, block), lambda i: (i, 0))],
        out_specs=pl.BlockSpec((half, block), lambda i: (i, 0)),
        out_shape=jax.ShapeDtypeStruct((2 * half, block), jnp.bfloat16),
        compiler_params=BIG,
        name="total",
    )(*grads_values, keep, sib, *more)


def combine_kernel(hi_ref, lo_ref, back_ref, out_ref):
    back = back_ref[...]
    value = jnp.dot(hi_ref[...], back, preferred_element_type=jnp.float32)
    value = value + jnp.dot(lo_ref[...], back, preferred_element_type=jnp.float32)
    out_ref[...] = value.astype(out_ref.dtype)


def combine(high, low, back):
    return pl.pallas_call(
        combine_kernel,
        out_shape=jax.ShapeDtypeStruct((high.shape[0], back.shape[1]), jnp.bfloat16),
        name="combine",
    )(high, low, back)


def exchange(rows, n_tok):
    blocks = rows.reshape(n_tok, rows.shape[0] // n_tok, rows.shape[1])
    return lax.all_to_all(blocks, "tok", split_axis=0, concat_axis=0, tiled=True).reshape(rows.shape)


def send(value, to):
    pairs = []
    for i in range(CHIPS * CORES):
        chip, core = to(i // CORES, i % CORES)
        pairs.append((i, chip % CHIPS * CORES + core))
    return lax.ppermute(value, "tp", pairs)


def from_near(value):
    return send(value, lambda chip, core: (chip + 1 - 2 * core, core))


def to_near(value):
    return send(value, lambda chip, core: (chip - 1 + 2 * core, core))


def to_near_other(value):
    return send(value, lambda chip, core: (chip - 1 + 2 * core, 1 - core))


def to_sibling(value):
    return send(value, lambda chip, core: (chip, 1 - core))


def block_order(chip, core):
    near = chip - 1 + 2 * core
    chips = jnp.stack([chip, near, near, chip + 2]) & (CHIPS - 1)
    return chips * CORES + jnp.stack([core, core, 1 - core, core])


def expert(own, weights):
    place = lax.axis_index("tp").astype(jnp.int32)
    chip, core = place >> 1, place & 1
    keep, give = pack(jnp.concatenate([block_order(chip, core), block_order(chip, 1 - core)]), weights)
    sib = to_sibling(give)
    half = own.shape[0] // 2
    halves = (own[:half], own[half:])
    same = [from_near(rows) for rows in halves]
    other = [to_near_other(rows) for rows in halves]
    opposite = [from_near(rows) for rows in same]
    mine = first(own, *same, keep, sib)
    values, more, other_parts = [], [], ()
    for part in range(2):
        rows = second(other[part], opposite[part], keep, sib, mine, part)
        value, for_opposite, for_other = grads(rows, to_sibling(rows), keep, sib, part, other_parts)
        other_parts = (for_other,)
        values.append(value)
        more.append(to_near(near(value, keep, sib, to_near(for_opposite))))
    return total(values, keep, sib, (*more, to_near_other(for_other)))


def shards(activations, out_grad, routes, gate_vals, w_gate, w_up, w_down):
    n_tok = lax.axis_size("tok")
    tok_dev, top_k = routes.shape
    capacity = max(2, 2 * tok_dev * top_k // n_tok)
    sent = dispatch(routes, activations, out_grad, n_tok, capacity)
    weights, sent, gate_vals = lax.optimization_barrier(((w_gate[0], w_up[0], w_down[0]), sent, gate_vals))
    high, low = mixer(routes, gate_vals, n_tok, capacity)
    own, high, low = lax.optimization_barrier((exchange(sent, n_tok), high, low))
    expert_sum = expert(own, weights)
    return combine(high, low, exchange(expert_sum, n_tok))


def solution(mesh):
    placed = (
        P("tok", "tp"),
        P("tok", "tp"),
        P("tok", None),
        P("tok", None),
        P("tok", "tp", None),
        P("tok", "tp", None),
        P("tok", "tp", None),
    )
    return jax.shard_map(
        shards, mesh=mesh, in_specs=placed, out_specs=P("tok", "tp"), check_vma=False
    )
```
